32 devices in a mesh: order: 1, shard: 32 (over z, y, x, core).
Axes of the slice: x: 2, y: 2, z: 4, core: 2. Of those that a mesh axis runs over, the one named last changes fastest.
Arguments:
- sky_coeffs: float32 [32, 2, 2048], P('shard'), may hold values from -6 to 6
- beam_coeffs: float32 [64, 2048], P('order'), may hold values from -0.09375 to 0.09375
- wigner: bfloat16 [32, 64, 2048, 128], P('shard', 'order'), may hold values from -0.125 to 0.125
- visits: int32 [32, 32, 4], P(('order', 'shard')), may hold values from -1 to 511, as said below
- point_slot: int32 [524288], P(('order', 'shard')), may hold values from 0 to 127, as said below
- phi_cell: int32 [524288], P(('order', 'shard')), may hold values from 0 to 30
- psi_cell: int32 [524288], P(('order', 'shard')), may hold values from 0 to 127
- fraction: float32 [2, 524288], P(None, ('order', 'shard')), may hold values from 0 to 1
Outputs:
- timeline: float32 [524288], P(('order', 'shard'))
The draws below stay inside these ranges and needn't reach their ends.
Inputs may be any that keep to these rules, and one draw needn't show every extreme that they name: Live entries of one row visits[r, d] are distinct tiles of owner d and come first; every row holds 1 to 4 live entries; for every device r some owner d has all 4 entries live. `point_slot`: every pointing names a live entry of its own device's visit list. Of one device's pointings, exactly 768 name each of half of the owners and 256 each of the others.
All inputs are finite; a program needn't handle non-finite values.
Results may differ from the reference program's by a relative error of at most 0.008.
Values may be sent and summed in bfloat16 or wider, within the bound.
A program may use at most 128 MiB of HBM per device.

```python
import math
import jax
import jax.numpy as jnp
from jax import lax

L = 2048
KBEAM = 64
NPHI = 4096
NPSI = 128
PHI_T = 32
SLOTS = 4
ROWS = 4
P_DEV = 16384
MTOT = 32
THETA = 128
PTOT = 524288
BLOCKS = 128
TPO = 512
N_ORDER = 1
N_SHARD = 32
DEVICES = 32


def visit_plan(key):
    base = jax.random.fold_in(key, 7)
    key_count, key_score, key_full = jax.random.split(base, 3)
    counts = jax.random.randint(key_count, (DEVICES, DEVICES), 1, SLOTS + 1)
    full_owner = jax.random.permutation(key_full, DEVICES)
    owners = jnp.arange(DEVICES, dtype=jnp.int32)[None, :]
    counts = jnp.where(owners == full_owner[:, None], SLOTS, counts)
    scores = jax.random.randint(key_score, (DEVICES, DEVICES, TPO), 0, 1048576) * TPO
    scores = scores + jnp.arange(TPO, dtype=jnp.int32)[None, None, :]
    picked = jnp.argsort(scores, axis=-1)[:, :, :SLOTS].astype(jnp.int32)
    live = jnp.arange(SLOTS, dtype=jnp.int32)[None, None, :] < counts[:, :, None]
    return (jnp.where(live, picked, -1).astype(jnp.int32), counts.astype(jnp.int32))


def draw_visits(key, part):
    table, counts = visit_plan(key)
    return table


def draw_point_slot(key, part):
    table, counts = visit_plan(key)
    key_perm, key_order, key_slot = jax.random.split(jax.random.fold_in(key, 11), 3)
    per_owner = P_DEV // DEVICES
    half = P_DEV // 2
    position = jnp.arange(P_DEV, dtype=jnp.int32)
    light = position % DEVICES
    heavy = (position - half) // per_owner
    rank_owner = jnp.where(position < half, light, heavy).astype(jnp.int32)
    perm_scores = jax.random.randint(key_perm, (DEVICES, DEVICES), 0, 65536) * DEVICES
    perm_scores = perm_scores + jnp.arange(DEVICES, dtype=jnp.int32)[None, :]
    owner_perm = jnp.argsort(perm_scores, axis=-1).astype(jnp.int32)
    owner_base = owner_perm[:, rank_owner]
    order_scores = jax.random.randint(key_order, (DEVICES, P_DEV), 0, 8192) * P_DEV
    order_scores = order_scores + position[None, :]
    shuffle = jnp.argsort(order_scores, axis=-1).astype(jnp.int32)
    owner = jnp.take_along_axis(owner_base, shuffle, axis=1).reshape(PTOT).astype(jnp.int32)
    device = jnp.arange(PTOT, dtype=jnp.int32) // P_DEV
    live_count = counts[device, owner]
    slot = jax.random.randint(key_slot, (PTOT,), 0, 65536) * live_count // 65536
    return (owner * SLOTS + slot).astype(jnp.int32)


def touch_ends(result, stream_key, least, top_value):
    place = [jax.random.randint(jax.random.fold_in(stream_key, axis), (), 0, length) for axis, length in enumerate(result.shape)]
    longest = result.shape.index(max(result.shape))
    next_to = place[:longest] + [(place[longest] + 1) % result.shape[longest]] + place[longest + 1:]
    return result.at[tuple(place)].set(least).at[tuple(next_to)].set(top_value)


def shard_levels(key, extent, shards, low, high):
    loudness = 1.0
    for axis_at, parts in shards:
        steps = jax.random.uniform(jax.random.fold_in(jax.random.fold_in(key, 6), axis_at), (parts,), jnp.float32, low / len(shards), high / len(shards))
        loudness = loudness * jnp.repeat(jnp.exp(steps), extent[axis_at] // parts).reshape((-1,) + (1,) * (len(extent) - 1 - axis_at))
    return loudness


def bell_draw(rng, dims, width, limit, shards=(), kind=jnp.bfloat16):
    result = width * jax.random.normal(rng, dims, jnp.float32)
    if shards:
        result = result * shard_levels(rng, dims, shards, -0.22, 0.18)
    return jnp.clip(result, -limit, limit).astype(kind)


def setup_inputs(seed: int = 0) -> dict:
    splits = jax.random.split(jax.random.key(seed), 9)
    sky_coeffs = bell_draw(splits[0], (MTOT, 2, L), 1.0, 6.0, ((0, 32),), jnp.float32)
    beam_coeffs = bell_draw(splits[1], (KBEAM, L), (2 * MTOT * KBEAM) ** -0.5, 0.09375, (), jnp.float32)
    wigner = bell_draw(splits[2], (MTOT, KBEAM, L, THETA), L ** -0.5, 0.125, ((0, 32),))
    visits = draw_visits(jax.random.fold_in(splits[8], 71), 0)
    point_slot = draw_point_slot(jax.random.fold_in(splits[8], 71), 0)
    phi_cell = touch_ends(jax.random.randint(splits[5], (PTOT,), 0, PHI_T - 1), jax.random.fold_in(splits[5], 1), 0, (PHI_T - 1) - 1).astype(jnp.int32)
    psi_cell = touch_ends(jax.random.randint(splits[6], (PTOT,), 0, NPSI), jax.random.fold_in(splits[6], 1), 0, NPSI - 1).astype(jnp.int32)
    fraction = jnp.clip(1.0 * jax.random.uniform(splits[7], (2, PTOT), jnp.float32) ** shard_levels(splits[7], (2, PTOT), ((1, 32),), -0.2, 0.2), 0.0, 1.0)
    return {"sky_coeffs": sky_coeffs, "beam_coeffs": beam_coeffs, "wigner": wigner, "visits": visits, "point_slot": point_slot, "phi_cell": phi_cell, "psi_cell": psi_cell, "fraction": fraction}


def wave_table(count, modes, first):
    grid = jnp.arange(count, dtype=jnp.int32)[:, None]
    mode = jnp.arange(modes, dtype=jnp.int32)[None, :] + first
    phase = ((grid * mode) % count).astype(jnp.float32) * (2.0 * math.pi / count)
    return jnp.cos(phase).astype(jnp.bfloat16), jnp.sin(phase).astype(jnp.bfloat16)


def reference(sky_coeffs, beam_coeffs, wigner, visits, point_slot, phi_cell, psi_cell, fraction):
    def mode_terms(pair):
        sky_mode, table_mode = pair
        weighted = (sky_mode[None, :, :] * beam_coeffs[:, None, :]).astype(jnp.bfloat16)
        terms = jnp.einsum("kcl,klt->tkc", weighted.astype(jnp.float32), table_mode.astype(jnp.float32))
        return terms.astype(jnp.bfloat16)

    coeffs = lax.map(mode_terms, (sky_coeffs, wigner))
    coeffs = jnp.transpose(coeffs, (1, 0, 2, 3))
    cos_phi, sin_phi = wave_table(NPHI, MTOT, 0)
    cos_psi, sin_psi = wave_table(NPSI, KBEAM, 0)
    group_orders = KBEAM // N_ORDER
    cos_group = jnp.transpose(cos_psi).reshape(N_ORDER, group_orders, NPSI).astype(jnp.float32)
    sin_group = jnp.transpose(sin_psi).reshape(N_ORDER, group_orders, NPSI).astype(jnp.float32)

    def theta_row(row):
        real_part = row[:, :, 0]
        imag_part = row[:, :, 1]
        synth_real = (jnp.dot(cos_phi, real_part, preferred_element_type=jnp.float32)
                      - jnp.dot(sin_phi, imag_part, preferred_element_type=jnp.float32)).astype(jnp.bfloat16)
        synth_imag = (jnp.dot(sin_phi, real_part, preferred_element_type=jnp.float32)
                      + jnp.dot(cos_phi, imag_part, preferred_element_type=jnp.float32)).astype(jnp.bfloat16)
        grouped_real = synth_real.reshape(NPHI, N_ORDER, group_orders).astype(jnp.float32)
        grouped_imag = synth_imag.reshape(NPHI, N_ORDER, group_orders).astype(jnp.float32)
        partial_value = (jnp.einsum("pok,okq->opq", grouped_real, cos_group)
                   - jnp.einsum("pok,okq->opq", grouped_imag, sin_group))
        rounded = lax.optimization_barrier(partial_value.astype(jnp.bfloat16)).astype(jnp.float32)
        return jnp.sum(rounded, axis=0).astype(jnp.bfloat16)

    cube = lax.map(theta_row, coeffs)
    flat_cube = cube.reshape(-1)
    device = (jnp.arange(PTOT, dtype=jnp.int32) // P_DEV).astype(jnp.int32)
    owner = point_slot // SLOTS
    tile = visits[device, owner, point_slot % SLOTS]
    owner_order = owner // N_SHARD
    owner_shard = owner % N_SHARD
    row_index = owner_shard * ROWS + tile // BLOCKS
    phi_index = owner_order * (NPHI // N_ORDER) + (tile % BLOCKS) * PHI_T + phi_cell
    next_psi = (psi_cell + 1) % NPSI
    base = row_index * (NPHI * NPSI) + phi_index * NPSI
    corner_aa = flat_cube[base + psi_cell].astype(jnp.float32)
    corner_ab = flat_cube[base + next_psi].astype(jnp.float32)
    corner_ba = flat_cube[base + NPSI + psi_cell].astype(jnp.float32)
    corner_bb = flat_cube[base + NPSI + next_psi].astype(jnp.float32)
    along_phi = fraction[0]
    along_psi = fraction[1]
    return ((1.0 - along_phi) * ((1.0 - along_psi) * corner_aa + along_psi * corner_ab)
            + along_phi * ((1.0 - along_psi) * corner_ba + along_psi * corner_bb))
```

```python
import functools
import math

import jax
import jax.numpy as jnp
import numpy as np
from jax import lax
from jax.experimental import pallas as pl
from jax.experimental.pallas import tpu as pltpu
from jax.sharding import PartitionSpec as P

NPHI = 4096
NPSI = 128
PHI_T = 32
LOW = 8
LANES = 128
CHUNK = 256
KB = 8
BLOCK = 256
F32, BF16, I32 = jnp.float32, jnp.bfloat16, jnp.int32


SQUARE = 4
CORES = 2


NT = (((1,), (1,)), ((), ()))


def hot(index, size):
    n = index.shape[1]
    return lax.broadcasted_iota(I32, (size, n), 0) == index


def wave(count, grid, mode):
    phase = 2.0 * math.pi * ((grid * mode) % count) / count
    return np.cos(phase), np.sin(phase)


def phi_matrix(modes):
    m = np.arange(modes)[None, :]
    cos, sin = wave(NPHI, np.arange(PHI_T)[:, None], m)
    eye = np.eye(KB)
    core = np.stack([np.stack([cos, -sin], -1), np.stack([sin, cos], -1)], 1)
    full = np.einsum("pamc,kj->pakmcj", core, eye)
    return jnp.asarray(full.reshape(PHI_T * 2 * KB, modes * 2 * KB), BF16)


def psi_matrix(orders):
    k = np.arange(orders)[None, :]
    cos, sin = wave(NPSI, np.arange(NPSI)[:, None], k)
    pair = np.stack([cos.reshape(NPSI, -1, KB), -sin.reshape(NPSI, -1, KB)], 2)
    return jnp.asarray(pair.reshape(NPSI, 2 * orders), BF16)


def rank_matrix():
    i = np.arange(BLOCK)
    upper = (i[:, None] < i[None, :]).astype(np.float32)
    return jnp.asarray(np.concatenate([upper, np.ones((BLOCK, LANES), np.float32)], 1), BF16)


def prepare(owners, depth, unit, slot_ref, phi_ref, psi_ref, frac_ref, rank_ref,
            dest_ref, sorted_ref, chunk_ref, carry, counts, stack, acc):
    blocks = slot_ref.shape[0]
    terms = 6

    def own(b):
        return hot(slot_ref[pl.ds(b, 1), :] // depth, owners)

    def count(b, total):
        return total + jnp.where(own(b), 1.0, 0.0)

    total = lax.fori_loop(0, blocks, count, jnp.zeros((owners, BLOCK), F32), unroll=4)
    ones = jnp.ones((BLOCK, LANES), BF16)
    units = jnp.dot(total.astype(BF16), ones, preferred_element_type=F32) * (1.0 / unit)
    below = (
        lax.broadcasted_iota(I32, (owners, owners), 0) > lax.broadcasted_iota(I32, (owners, owners), 1)
    ).astype(F32).astype(BF16)
    start = jnp.dot(below, units.astype(BF16), preferred_element_type=F32)
    lane = lax.broadcasted_iota(I32, (owners, LANES), 1).astype(F32)
    chunk_ref[...] = jnp.sum(jnp.where(start + units <= lane, 1.0, 0.0), axis=0, keepdims=True).astype(I32)
    carry[...] = start * unit

    def rank(b, c):
        mask = own(b)
        found = jnp.dot(jnp.where(mask, 1.0, 0.0).astype(BF16), rank_ref[...], preferred_element_type=F32)
        base = carry[...]
        spot = found[:, :BLOCK] + jnp.concatenate([base] * (BLOCK // LANES), axis=1)
        dest_ref[pl.ds(b, 1), :] = jnp.sum(jnp.where(mask, spot, 0.0), axis=0, keepdims=True).astype(I32)
        carry[...] = base + found[:, BLOCK:]
        return c

    lax.fori_loop(0, blocks, rank, 0, unroll=2)
    acc[...] = jnp.zeros_like(acc)
    group = 4

    def move(g, c):
        rows, lanes = [], []
        for u in range(group):
            b = g * group + u
            dest = dest_ref[pl.ds(b, 1), :]
            slot = slot_ref[pl.ds(b, 1), :]
            at = (phi_ref[pl.ds(b, 1), :] * depth + slot % depth).astype(F32)
            psi = psi_ref[pl.ds(b, 1), :].astype(F32)
            along, across = frac_ref[0, pl.ds(b, 1), :], frac_ref[1, pl.ds(b, 1), :]
            along_c, across_c = along.astype(BF16).astype(F32), across.astype(BF16).astype(F32)
            row = hot(dest // LANES, LANES)
            parts = [at, psi, along_c, along - along_c, across_c, across - across_c]
            rows.append(jnp.concatenate([jnp.where(row, p, 0.0).astype(BF16) for p in parts], axis=0))
            lanes.append(jnp.where(hot(dest % LANES, LANES), 1.0, 0.0).astype(BF16))
        acc[...] += lax.dot_general(
            jnp.concatenate(rows, axis=1), jnp.concatenate(lanes, axis=1), NT, preferred_element_type=F32
        )
        return c

    lax.fori_loop(0, blocks // group, move, 0)
    r = LANES
    sorted_ref[0] = acc[0:r]
    sorted_ref[1] = acc[r:2 * r]
    sorted_ref[2] = acc[2 * r:3 * r] + acc[3 * r:4 * r]
    sorted_ref[3] = acc[4 * r:5 * r] + acc[5 * r:6 * r]


def convolve(modes, orders, owners, depth, chunk_ref, coeffs_ref, visit_ref, phi_mat, psi_mat,
             sorted_ref, dest_ref, out_ref, synth, lines, table, found):
    slots = owners * depth
    theta = coeffs_ref.shape[1]
    blocks = NPHI // PHI_T
    steps = orders // KB
    wide = 2 * KB
    tile = jnp.maximum(jnp.concatenate([visit_ref[d:d + 1, :] for d in range(depth)], axis=1), 0)
    owner = lax.broadcasted_iota(I32, (1, slots), 1) % owners
    row = owner * (theta // owners) + tile // blocks
    first = (tile % blocks) * PHI_T
    pick = jnp.where(hot(row, theta), 1.0, 0.0).astype(BF16)
    turn = (lax.broadcasted_iota(I32, (modes, slots), 0) * first) % NPHI
    angle = turn.astype(F32) * (2.0 * math.pi / NPHI)
    cos, sin = jnp.cos(angle), jnp.sin(angle)

    def step(j, c):
        rows = jnp.concatenate(
            [coeffs_ref[pl.ds(pl.multiple_of(m * 2 * orders + j * wide, wide), wide), :] for m in range(modes)], axis=0
        )
        x = jnp.dot(rows, pick, preferred_element_type=F32)
        turned = []
        for m in range(modes):
            re, im = x[m * wide:m * wide + KB], x[m * wide + KB:(m + 1) * wide]
            cm, sm = cos[m:m + 1], sin[m:m + 1]
            turned.append(jnp.concatenate([cm * re - sm * im, sm * re + cm * im], axis=0).astype(BF16))
        y = jnp.dot(phi_mat[...], jnp.concatenate(turned, axis=0), preferred_element_type=F32)
        for p in range(PHI_T):
            synth[p, pl.ds(pl.multiple_of(j * wide, wide), wide), :] = y[p * wide:(p + 1) * wide].astype(BF16)
        return c

    lax.fori_loop(0, steps, step, 0)
    eye = (
        lax.broadcasted_iota(I32, (slots, slots), 0) == lax.broadcasted_iota(I32, (slots, slots), 1)
    ).astype(F32).astype(BF16)

    def flip(p, c):
        lines[pl.ds(pl.multiple_of(p * slots, slots), slots), :] = lax.dot_general(
            eye, synth[p], NT, preferred_element_type=F32)
        return c

    lax.fori_loop(0, PHI_T, flip, 0, unroll=4)

    def cube(o, c):
        part = lines[pl.ds(o, PHI_T * depth, stride=owners), :].astype(BF16)
        t = lax.dot_general(psi_mat[...], part, NT, preferred_element_type=F32).astype(BF16)
        table[pl.ds(pl.multiple_of(o * NPSI, NPSI), NPSI), :] = jnp.concatenate([t, t], axis=1)
        return c

    lax.fori_loop(0, owners, cube, 0, unroll=4)
    per = BLOCK // LANES

    def wide_row(i, c):
        return jnp.concatenate([sorted_ref[i, pl.ds(c * per + u, 1), :] for u in range(per)], axis=1)

    def chunk(c, s):
        o = chunk_ref[0, c]
        at, psi = wide_row(0, c).astype(I32), wide_row(1, c).astype(I32)
        along, across = wide_row(2, c), wide_row(3, c)
        spots = lax.broadcasted_iota(I32, (PHI_T * depth, BLOCK), 0)
        w = jnp.where(spots == at, 1.0 - along, jnp.where(spots == at + depth, along, 0.0))
        coarse = w.astype(BF16)
        fine = (w - coarse.astype(F32)).astype(BF16)
        t = table[pl.ds(pl.multiple_of(o * NPSI, NPSI), NPSI), :]
        g = jnp.dot(t, jnp.concatenate([coarse, fine], axis=0), preferred_element_type=F32)
        angles = lax.broadcasted_iota(I32, (NPSI, BLOCK), 0)
        v = jnp.where(angles == psi, 1.0 - across, jnp.where(angles == (psi + 1) % NPSI, across, 0.0))
        line = jnp.sum(g * v, axis=0, keepdims=True)
        for u in range(per):
            found[pl.ds(c * per + u, 1), :] = line[:, u * LANES:(u + 1) * LANES]
        return s

    count = dest_ref.shape[0]
    lax.fori_loop(0, count, chunk, 0, unroll=2)
    values = found[...]
    coarse = values.astype(BF16)
    fine = (values - coarse.astype(F32)).astype(BF16)
    both = jnp.concatenate([coarse, fine], axis=1)

    def back(b, s):
        dest = dest_ref[pl.ds(b, 1), :]
        lanes = jnp.where(hot(dest % LANES, LANES), 1.0, 0.0).astype(BF16)
        h = jnp.dot(both, jnp.concatenate([lanes, lanes], axis=0), preferred_element_type=F32)
        out_ref[pl.ds(b, 1), :] = jnp.sum(jnp.where(hot(dest // LANES, LANES), h, 0.0), axis=0, keepdims=True)
        return s

    lax.fori_loop(0, count, back, 0, unroll=2)


V = pl.BlockSpec(memory_space=pltpu.VMEM)


def run_prepare(point_slot, phi_cell, psi_cell, fraction, owners, depth):
    count = point_slot.shape[0]
    blocks = count // BLOCK
    unit = count // owners // 2
    return pl.pallas_call(
        functools.partial(prepare, owners, depth, unit),
        out_shape=(
            jax.ShapeDtypeStruct((blocks, BLOCK), I32),
            jax.ShapeDtypeStruct((4, LANES, LANES), F32),
            jax.ShapeDtypeStruct((1, LANES), I32),
        ),
        in_specs=[V] * 5,
        out_specs=(V, V, V),
        scratch_shapes=[
            pltpu.VMEM((owners, LANES), F32),
            pltpu.VMEM((owners, LANES), F32),
            pltpu.VMEM((8, LANES), F32),
            pltpu.VMEM((6 * LANES, LANES), F32),
        ],
        name="prepare",
    )(point_slot.reshape(blocks, BLOCK), phi_cell.reshape(blocks, BLOCK), psi_cell.reshape(blocks, BLOCK),
      fraction.reshape(2, blocks, BLOCK), rank_matrix())


def run_convolve(coeffs, visits, dest, spots, chunks, modes, orders):
    owners, depth = visits.shape
    slots = owners * depth
    return pl.pallas_call(
        functools.partial(convolve, modes, orders, owners, depth),
        out_shape=jax.ShapeDtypeStruct(dest.shape, F32),
        in_specs=[pl.BlockSpec(memory_space=pltpu.SMEM)] + [V] * 6,
        out_specs=V,
        scratch_shapes=[
            pltpu.VMEM((PHI_T, 2 * orders, slots), BF16),
            pltpu.VMEM((PHI_T * slots, 2 * orders), F32),
            pltpu.VMEM((owners * NPSI, 2 * LANES), BF16),
            pltpu.VMEM((LANES, LANES), F32),
        ],
        name="convolve",
    )(chunks, coeffs, jnp.transpose(visits), phi_matrix(modes), psi_matrix(orders), spots, dest)

def grouped(order_count, visits, count):
    owners, depth = visits[1:]
    return order_count == 1 and owners * depth == LANES and count == LANES * LANES and count % (2 * owners * BLOCK) == 0


def gather_blocks(lines, block_ref, out_ref, send_sem, recv_sem):
    me = lax.axis_index("shard")
    core = me % CORES
    square = me // CORES % SQUARE
    line = me // (CORES * SQUARE)
    depth = block_ref.shape[0]

    def index(at_line, at_square, at_core):
        return (at_line * SQUARE + at_square) * CORES + at_core

    along = [(line + d) % lines for d in range(1, lines)]
    if lines == 4:
        half = line // 2
        along = [line + 1 - 2 * (line % 2), 2 - half, 3 - 3 * half]
    across = [(square + d) % SQUARE for d in range(1, SQUARE)]
    other = (core + 1) % CORES
    line_peers = [index(a, square, core) for a in along]
    square_peers = [index(line, b, core) for b in across]
    twin = index(line, square, other)
    barrier = pltpu.get_barrier_semaphore()
    peers = line_peers + square_peers + [twin]
    for peer in peers:
        pl.semaphore_signal(
            barrier, inc=1, device_id={"shard": peer}, device_id_type=pl.DeviceIdType.MESH
        )
    pl.semaphore_wait(barrier, len(peers))

    started = []

    def place(owner):
        return out_ref.at[pl.ds(pl.multiple_of(owner * depth, depth), depth), :]

    def send(source, owner, peer):
        copy = pltpu.make_async_remote_copy(
            src_ref=source,
            dst_ref=place(owner),
            send_sem=send_sem.at[len(started)],
            recv_sem=recv_sem.at[owner],
            device_id={"shard": peer},
            device_id_type=pl.DeviceIdType.MESH,
        )
        copy.start()
        started.append(copy)

    def arrive(owner):
        pltpu.make_async_remote_copy(
            src_ref=place(owner),
            dst_ref=place(owner),
            send_sem=send_sem.at[0],
            recv_sem=recv_sem.at[owner],
            device_id={"shard": twin},
            device_id_type=pl.DeviceIdType.MESH,
        ).wait_recv()

    for peer in line_peers[::-1] + square_peers + [twin]:
        send(block_ref, me, peer)
    out_ref[pl.ds(pl.multiple_of(me * depth, depth), depth), :] = block_ref[...]
    for owner in line_peers:
        arrive(owner)
        for peer in square_peers + [twin]:
            send(place(owner), owner, peer)
    for a in [line] + along:
        for b in across:
            owner = index(a, b, core)
            arrive(owner)
            send(place(owner), owner, twin)
    for a in [line] + along:
        for b in [square] + across:
            arrive(index(a, b, other))
    for copy in started:
        copy.wait_send()


def wave_table(count, grid, mode):
    phase = 2.0 * math.pi * ((grid * mode) % count) / count
    return np.cos(phase), np.sin(phase)


def interpolate(
    modes,
    orders,
    order_count,
    shard_count,
    coeffs_ref,
    visit_ref,
    phi_table_ref,
    psi_table_ref,
    slot_ref,
    phi_ref,
    psi_ref,
    fraction_ref,
    out_ref,
    picked,
    edge,
    synth,
    wave_a,
    wave_b,
    values_a,
    values_b,
):
    terms = 2 * orders
    high = PHI_T // LOW
    theta = coeffs_ref.shape[1]
    depth, owners = visit_ref.shape
    slots = owners * depth
    blocks = NPHI // (order_count * PHI_T)
    groups = slots // LANES
    listed = jnp.concatenate([visit_ref[d : d + 1, :] for d in range(depth)], axis=1)
    for g in range(groups):
        lanes = slice(g * LANES, (g + 1) * LANES)
        tile = jnp.maximum(listed[:, lanes], 0)
        owner = (lax.broadcasted_iota(jnp.int32, (1, LANES), 1) + g * LANES) % owners
        row = (owner % shard_count) * (theta // shard_count) + tile // blocks
        first_phi = (owner // shard_count) * (NPHI // order_count) + (tile % blocks) * PHI_T
        chosen = (
            lax.broadcasted_iota(jnp.int32, (theta, LANES), 0) == row
        ).astype(jnp.float32).astype(jnp.bfloat16)

        def pick(m, carry):
            rows = pl.ds(pl.multiple_of(m * 4 * terms, 4 * terms), 4 * terms)
            picked[rows, :] = jnp.dot(
                coeffs_ref[rows, :], chosen, preferred_element_type=jnp.float32
            )
            return carry

        lax.fori_loop(0, modes // 4, pick, 0)
        turn = (lax.broadcasted_iota(jnp.int32, (modes, LANES), 0) * first_phi) % NPHI
        angle = turn.astype(jnp.float32) * (2.0 * math.pi / NPHI)
        turn_cos, turn_sin = jnp.cos(angle), jnp.sin(angle)

        def sum_modes(k, carry):
            real = picked[pl.ds(2 * k, modes, stride=terms), :]
            imag = picked[pl.ds(2 * k + 1, modes, stride=terms), :]
            turned = jnp.concatenate(
                [turn_cos * real - turn_sin * imag, turn_sin * real + turn_cos * imag], axis=0
            ).astype(jnp.bfloat16)
            values = jnp.dot(phi_table_ref[...], turned, preferred_element_type=jnp.float32)
            for h in range(high):
                synth[
                    pl.ds(pl.multiple_of(k * 2 * LOW, 2 * LOW), 2 * LOW),
                    h * slots + g * LANES : h * slots + (g + 1) * LANES,
                ] = values[h * 2 * LOW : (h + 1) * 2 * LOW].astype(jnp.bfloat16)
            edge[pl.ds(pl.multiple_of(k * 2 * high, 2 * high), 2 * high), :] = values[
                2 * PHI_T :
            ]
            return carry

        lax.fori_loop(0, orders, sum_modes, 0, unroll=4)
        for part in range(2):
            for h in range(high):
                synth[
                    terms * LOW + part * orders : terms * LOW + (part + 1) * orders,
                    h * slots + g * LANES : h * slots + (g + 1) * LANES,
                ] = edge[pl.ds(part * high + h, orders, stride=2 * high), :].astype(jnp.bfloat16)

    def begin(i, values, wave):
        phi, psi = phi_ref[i], psi_ref[i]
        along_psi = fraction_ref[i][1:2]
        slot = slot_ref[i]
        key = ((phi // LOW) * depth + slot % depth) * owners + slot // depth
        entry = (
            lax.broadcasted_iota(jnp.int32, (high * slots, CHUNK), 0) == key
        ).astype(jnp.float32).astype(jnp.bfloat16)
        at_psi = lax.broadcasted_iota(jnp.int32, (NPSI, CHUNK), 0)
        weight = jnp.where(
            at_psi == psi, 1.0 - along_psi, jnp.where(at_psi == (psi + 1) % NPSI, along_psi, 0.0)
        )
        coarse = weight.astype(jnp.bfloat16)
        fine = (weight - coarse.astype(jnp.float32)).astype(jnp.bfloat16)
        wave[...] = jnp.dot(
            psi_table_ref[...],
            jnp.concatenate([coarse, fine], axis=0),
            preferred_element_type=jnp.float32,
        )
        values[...] = jnp.dot(synth[...], entry, preferred_element_type=jnp.float32)

    def finish(i, values, wave):
        phi = phi_ref[i]
        along_phi = fraction_ref[i][0:1]
        sums = [jnp.zeros((LOW, CHUNK), jnp.float32) for _ in range(4)]
        for k in range(orders):
            for part in range(2):
                at = (2 * k + part) * LOW
                line = part * orders + k
                sums[at // LOW % 4] += values[at : at + LOW, :] * wave[line : line + 1, :]
        inner = (sums[0] + sums[1]) + (sums[2] + sums[3])
        last = jnp.sum(values[terms * LOW :, :] * wave[...], axis=0, keepdims=True)
        low = phi % LOW
        at_low = lax.broadcasted_iota(jnp.int32, (LOW, CHUNK), 0)
        weight_phi = jnp.where(
            at_low == low, 1.0 - along_phi, jnp.where(at_low == low + 1, along_phi, 0.0)
        )
        total = jnp.sum(inner * weight_phi, axis=0, keepdims=True)
        out_ref[i] = total + jnp.where(low == LOW - 1, along_phi, 0.0) * last

    chunks = slot_ref.shape[0]
    begin(0, values_a, wave_a)

    def pair(i, carry):
        begin(2 * i + 1, values_b, wave_b)
        finish(2 * i, values_a, wave_a)
        begin(jnp.minimum(2 * i + 2, chunks - 1), values_a, wave_a)
        finish(2 * i + 1, values_b, wave_b)
        return carry

    lax.fori_loop(0, chunks // 2, pair, 0)


def phi_rows(modes):
    mode = np.arange(modes, dtype=np.int64)[None, :]
    high = PHI_T // LOW
    cos, sin = wave_table(NPHI, np.arange(PHI_T, dtype=np.int64)[:, None], mode)
    real = np.concatenate([cos, -sin], axis=1)
    imag = np.concatenate([sin, cos], axis=1)
    inner = np.stack(
        [real.reshape(high, LOW, 2 * modes), imag.reshape(high, LOW, 2 * modes)], axis=1
    ).reshape(2 * PHI_T, 2 * modes)
    zero = np.zeros((1, 2 * modes), np.float64)
    edge = np.concatenate([real[LOW::LOW], zero, imag[LOW::LOW], zero], axis=0)
    return jnp.asarray(np.concatenate([inner, edge], axis=0), jnp.bfloat16)


def psi_rows(orders):
    order = np.arange(orders, dtype=np.int64)[:, None]
    cos, sin = wave_table(NPSI, np.arange(NPSI, dtype=np.int64)[None, :], order)
    half = np.concatenate([cos, -sin], axis=0)
    return jnp.asarray(np.concatenate([half, half], axis=1), jnp.bfloat16)


def shards(sky_coeffs, beam_coeffs, wigner, visits, point_slot, phi_cell, psi_cell, fraction):
    order_count = lax.axis_size("order")
    shard_count = lax.axis_size("shard")
    local_modes = sky_coeffs.shape[0]
    local_orders = beam_coeffs.shape[0]
    theta_count = wigner.shape[3]
    orders = local_orders * order_count
    modes = local_modes * shard_count
    weighted = (sky_coeffs[:, None, :, :] * beam_coeffs[None, :, None, :]).astype(jnp.bfloat16)
    coeffs = jnp.einsum("mkcl,mklt->mkct", weighted, wigner, preferred_element_type=jnp.float32)
    coeffs = coeffs.astype(jnp.bfloat16)
    if grouped(order_count, visits.shape, point_slot.shape[0]):
        coeffs = coeffs.reshape(local_modes, orders // KB, KB, 2, theta_count).transpose(0, 1, 3, 2, 4)
    coeffs = coeffs.reshape(local_modes * local_orders * 2, theta_count)
    coeffs = pl.pallas_call(
        functools.partial(gather_blocks, shard_count // (SQUARE * CORES)),
        out_shape=jax.ShapeDtypeStruct((shard_count * coeffs.shape[0], theta_count), jnp.bfloat16),
        in_specs=[pl.BlockSpec(memory_space=pltpu.VMEM)],
        out_specs=pl.BlockSpec(memory_space=pltpu.VMEM),
        scratch_shapes=[
            pltpu.SemaphoreType.DMA((shard_count - 1,)),
            pltpu.SemaphoreType.DMA((shard_count,)),
        ],
        compiler_params=pltpu.CompilerParams(collective_id=0, has_side_effects=True),
    )(coeffs)
    if order_count > 1:
        coeffs = coeffs.reshape(modes, local_orders * 2, theta_count)
        coeffs = lax.all_gather(coeffs, "order", axis=1, tiled=True)
        coeffs = coeffs.reshape(modes * orders * 2, theta_count)

    slots = visits.shape[1] * visits.shape[2]
    count = point_slot.shape[0]
    owners, depth = visits.shape[1:]
    unit = count // (2 * owners)
    if grouped(order_count, visits.shape, count):
        dest, spots, chunks = run_prepare(point_slot, phi_cell, psi_cell, fraction, owners, depth)
        return run_convolve(coeffs, visits[0], dest, spots, chunks, modes, orders).reshape(count)
    chunks = count // CHUNK
    lined = (chunks, 1, CHUNK)
    pairs = jnp.transpose(fraction.reshape(2, chunks, CHUNK), (1, 0, 2))
    high = PHI_T // LOW
    timeline = pl.pallas_call(
        functools.partial(
            interpolate, modes, orders, order_count, shard_count
        ),
        out_shape=jax.ShapeDtypeStruct(lined, jnp.float32),
        in_specs=[pl.BlockSpec(memory_space=pltpu.VMEM)] * 8,
        out_specs=pl.BlockSpec(memory_space=pltpu.VMEM),
        scratch_shapes=[
            pltpu.VMEM((modes * orders * 2, LANES), jnp.float32),
            pltpu.VMEM((orders * 2 * high, LANES), jnp.float32),
            pltpu.VMEM((orders * 2 * (LOW + 1), high * slots), jnp.bfloat16),
            pltpu.VMEM((orders * 2, CHUNK), jnp.float32),
            pltpu.VMEM((orders * 2, CHUNK), jnp.float32),
            pltpu.VMEM((orders * 2 * (LOW + 1), CHUNK), jnp.float32),
            pltpu.VMEM((orders * 2 * (LOW + 1), CHUNK), jnp.float32),
        ],
    )(
        coeffs,
        jnp.transpose(visits[0]),
        phi_rows(modes),
        psi_rows(orders),
        point_slot.reshape(lined),
        phi_cell.reshape(lined),
        psi_cell.reshape(lined),
        pairs,
    )
    return timeline.reshape(count)


def solution(mesh):
    placed = (
        P("shard", None, None),
        P("order", None),
        P("shard", "order", None, None),
        P(("order", "shard"), None, None),
        P(("order", "shard")),
        P(("order", "shard")),
        P(("order", "shard")),
        P(None, ("order", "shard")),
    )
    return jax.shard_map(
        shards, mesh=mesh, in_specs=placed, out_specs=P(("order", "shard")), check_vma=False
    )
```

```python
import functools
import math

import jax
import jax.numpy as jnp
import numpy as np
from jax import lax
from jax.experimental import pallas as pl
from jax.experimental.pallas import tpu as pltpu
from jax.sharding import PartitionSpec as P

NPHI = 4096
NPSI = 128
PHI_T = 32
LOW = 8
LANES = 128
CHUNK = 256
KB = 8
BLOCK = 256
F32, BF16, I32 = jnp.float32, jnp.bfloat16, jnp.int32


SQUARE = 4
CORES = 2


def gather_blocks(lines, block_ref, out_ref, send_sem, recv_sem):
    me = lax.axis_index("shard")
    core = me % CORES
    square = me // CORES % SQUARE
    line = me // (CORES * SQUARE)
    depth = block_ref.shape[0]

    def index(at_line, at_square, at_core):
        return (at_line * SQUARE + at_square) * CORES + at_core

    along = [(line + d) % lines for d in range(1, lines)]
    if lines == 4:
        half = line // 2
        along = [line + 1 - 2 * (line % 2), 2 - half, 3 - 3 * half]
    across = [(square + d) % SQUARE for d in range(1, SQUARE)]
    other = (core + 1) % CORES
    line_peers = [index(a, square, core) for a in along]
    square_peers = [index(line, b, core) for b in across]
    twin = index(line, square, other)
    barrier = pltpu.get_barrier_semaphore()
    peers = line_peers + square_peers + [twin]
    for peer in peers:
        pl.semaphore_signal(
            barrier, inc=1, device_id={"shard": peer}, device_id_type=pl.DeviceIdType.MESH
        )
    pl.semaphore_wait(barrier, len(peers))

    started = []

    def place(owner):
        return out_ref.at[pl.ds(pl.multiple_of(owner * depth, depth), depth), :]

    def send(source, owner, peer):
        copy = pltpu.make_async_remote_copy(
            src_ref=source,
            dst_ref=place(owner),
            send_sem=send_sem.at[len(started)],
            recv_sem=recv_sem.at[owner],
            device_id={"shard": peer},
            device_id_type=pl.DeviceIdType.MESH,
        )
        copy.start()
        started.append(copy)

    def arrive(owner):
        pltpu.make_async_remote_copy(
            src_ref=place(owner),
            dst_ref=place(owner),
            send_sem=send_sem.at[0],
            recv_sem=recv_sem.at[owner],
            device_id={"shard": twin},
            device_id_type=pl.DeviceIdType.MESH,
        ).wait_recv()

    for peer in line_peers[::-1] + square_peers + [twin]:
        send(block_ref, me, peer)
    out_ref[pl.ds(pl.multiple_of(me * depth, depth), depth), :] = block_ref[...]
    for owner in line_peers:
        arrive(owner)
        for peer in square_peers + [twin]:
            send(place(owner), owner, peer)
    for a in [line] + along:
        for b in across:
            owner = index(a, b, core)
            arrive(owner)
            send(place(owner), owner, twin)
    for a in [line] + along:
        for b in [square] + across:
            arrive(index(a, b, other))
    for copy in started:
        copy.wait_send()


def wave_table(count, grid, mode):
    phase = 2.0 * math.pi * ((grid * mode) % count) / count
    return np.cos(phase), np.sin(phase)


PARTS = 4
AHEAD = 2
LAG = (3, 5)
NT = (((1,), (1,)), ((), ()))


def grouped(lines, order_count, modes, orders, visits, count, theta):
    owners, depth = visits
    return (
        lines > 1
        and order_count == 1
        and modes == owners
        and orders % KB == 0
        and 2 * orders == theta == owners * depth == PHI_T * depth == NPSI == LANES
        and count % (2 * owners * BLOCK) == 0
        and count == orders * BLOCK
    )


def row_hot(index, size, dtype=BF16):
    n = index.shape[1]
    rows = lax.broadcasted_iota(I32, (size, n), 0)
    if dtype == BF16:
        return rows.astype(F32).astype(BF16) == jnp.broadcast_to(index.astype(F32).astype(BF16), (size, n))
    return rows == index


def pick_row(index, *values):
    size, n = values[0].shape
    totals = [jnp.zeros((8, n), F32) for _ in values]
    index = jnp.broadcast_to(index, (8, n)) - lax.broadcasted_iota(I32, (8, n), 0)
    for r in range(0, size, 8):
        mask = index == r
        totals = [jnp.where(mask, v[r:r + 8], t) for v, t in zip(values, totals)]
    return jnp.sum(functools.reduce(jnp.add, totals), axis=0, keepdims=True)


def block_of(ref, b):
    per = BLOCK // LANES
    return jnp.concatenate([ref[pl.ds(b * per + u, 1), :] for u in range(per)], axis=1)


def mode_order(modes):
    lines = modes // (SQUARE * CORES)
    place = np.arange(modes)
    return (place % lines) * SQUARE * CORES + place // lines % SQUARE * CORES + place // (lines * SQUARE)


def phi_matrix(modes):
    cos, sin = wave_table(NPHI, np.arange(PHI_T)[:, None], mode_order(modes)[None, :])
    core = np.stack([np.stack([cos, -sin], -1), np.stack([sin, cos], -1)], 1)
    full = np.einsum("pamc,kj->pakmcj", core, np.eye(KB))
    return jnp.asarray(full.reshape(PHI_T * 2 * KB, modes * 2 * KB), BF16)


def psi_matrix(orders):
    cos, sin = wave_table(NPSI, np.arange(NPSI)[:, None], np.arange(orders)[None, :])
    pair = np.stack([cos.reshape(NPSI, -1, KB), -sin.reshape(NPSI, -1, KB)], 2)
    return jnp.asarray(pair.reshape(NPSI, 2 * orders), BF16)


def rank_matrix():
    i = np.arange(BLOCK)
    upper = (i[:, None] < i[None, :]).astype(np.float32)
    return jnp.asarray(np.concatenate([upper, np.ones((BLOCK, LANES), np.float32)], 1), BF16)


class Ring:
    def __init__(self, shards, mine, out, send_sem, recv_sem):
        lines = shards // (SQUARE * CORES)
        me = lax.axis_index("shard")
        core, square, line = me % CORES, me // CORES % SQUARE, me // (CORES * SQUARE)
        index = lambda a, b, c: (a * SQUARE + b) * CORES + c
        along = [(line + d) % lines for d in range(1, lines)]
        across = [(square + d) % SQUARE for d in range(1, SQUARE)]
        other = (core + 1) % CORES
        self.shards, self.lines = shards, lines
        self.line_peers = [index(a, square, core) for a in along]
        self.square_peers = [index(line, b, core) for b in across]
        self.twin = index(line, square, other)
        self.all_peers = [
            index(a, b, c) for a in along[::-1] + [line] for b in across[::-1] + [square] for c in (other, core)
        ][:-1]
        self.mine, self.out, self.send_sem, self.recv_sem = mine, out, send_sem, recv_sem
        self.wide = mine.shape[1]
        self.column = core * SQUARE + square
        self.columns = [core * SQUARE + b for b in across]
        self.spot = self.column * lines + line

    def greet(self):
        barrier = pltpu.get_barrier_semaphore()
        for peer in self.all_peers:
            pl.semaphore_signal(barrier, inc=1, device_id={"shard": peer}, device_id_type=pl.DeviceIdType.MESH)
        pl.semaphore_wait(barrier, len(self.all_peers))

    def place(self, j, first, count):
        return self.out.at[j, pl.ds(pl.multiple_of(first * self.wide, self.wide), count * self.wide), :]

    def copy(self, source, target, j, peer, kind):
        return pltpu.make_async_remote_copy(
            src_ref=source,
            dst_ref=target,
            send_sem=self.send_sem.at[j],
            recv_sem=self.recv_sem.at[kind, j],
            device_id={"shard": peer},
            device_id_type=pl.DeviceIdType.MESH,
        )

    def arrive(self, j, kind, blocks):
        span = self.place(j, 0, blocks)
        self.copy(span, span, j, self.twin, kind).wait_recv()

    def sent(self, j, blocks):
        span = self.place(j, 0, blocks)
        self.copy(span, span, j, self.twin, 0).wait_send()

    def first(self, j):
        for peer in self.line_peers:
            self.copy(self.mine.at[j], self.place(j, self.spot, 1), j, peer, 0).start()

    def second(self, j):
        self.arrive(j, 0, self.lines - 1)
        span = self.place(j, self.column * self.lines, self.lines)
        for peer in self.square_peers:
            self.copy(span, span, j, peer, 1).start()
        self.copy(span, span, j, self.twin, 2).start()

    def third(self, j):
        self.arrive(j, 1, (SQUARE - 1) * self.lines)
        for column in self.columns:
            span = self.place(j, column * self.lines, self.lines)
            self.copy(span, span, j, self.twin, 2).start()

    def last(self, j):
        self.arrive(j, 2, SQUARE * self.lines)
        self.sent(j, self.lines - 1)
        self.sent(j, (2 * SQUARE - 1) * self.lines)

    def direct(self, j):
        for peer in self.all_peers:
            self.copy(self.mine.at[j], self.place(j, self.spot, 1), j, peer, 0).start()

    def direct_end(self, j):
        self.arrive(j, 0, self.shards - 1)

    def direct_sent(self, j):
        self.sent(j, self.shards - 1)


def whole_kernel(
    shards, owners, depth,
    sky_hbm, beam_hbm, wigner_hbm, visit_hbm, slot_hbm, phi_hbm, psi_hbm, fraction_hbm, phi_mat_hbm, psi_mat_hbm, rank_hbm,
    out_ref,
    sky, beam, wigner, visit, slot, phi, psi, fraction, phi_mat, psi_mat, rank_mat,
    gathered, mine, turn_cos, turn_sin, dest, carry, chunk_vmem, chunk_smem, moved, hot, weights, aims, synth, lines, table, found, found_both, *rest,
):
    *buffers, load_sem, small_sem, chunk_sem, send_sem, recv_sem = rest
    steps, wide = mine.shape[0], mine.shape[1]
    modes = shards
    theta = wigner.shape[2]
    slots = owners * depth
    blocks = found.shape[0]
    tiles = NPHI // PHI_T
    ring = Ring(shards, mine, gathered, send_sem, recv_sem)

    small = [
        (sky_hbm, sky), (beam_hbm, beam), (slot_hbm, slot), (visit_hbm, visit), (rank_hbm, rank_mat),
        (phi_hbm, phi), (psi_hbm, psi), (fraction_hbm, fraction), (phi_mat_hbm, phi_mat), (psi_mat_hbm, psi_mat),
    ]
    small = [pltpu.make_async_copy(s, d, small_sem.at[n]) for n, (s, d) in enumerate(small)]

    def load(j):
        rows = pl.ds(j * KB, KB)
        return pltpu.make_async_copy(wigner_hbm.at[rows], wigner.at[rows], load_sem.at[j])

    for copy in small[:4]:
        copy.start()
    load(0).start()
    for copy in small[4:]:
        copy.start()
    ahead = AHEAD
    for j in range(1, ahead):
        load(j).start()
    ring.greet()

    small[2].wait()

    def own(b):
        owner = block_of(slot, b) >> int(math.log2(depth))
        return lax.broadcasted_iota(I32, (owners, BLOCK), 0) == owner

    def count(b, total):
        return total + jnp.where(own(b), 1, 0)

    total = lax.fori_loop(0, blocks, count, jnp.zeros((owners, BLOCK), I32), unroll=8)
    held = jnp.broadcast_to(jnp.sum(total, axis=1, keepdims=True), (owners, LANES))
    place = lax.broadcasted_iota(I32, (owners, LANES), 0)
    start = jnp.zeros((owners, LANES), I32)
    for o in range(owners - 1):
        start = start + jnp.where(place > o, jnp.broadcast_to(held[o:o + 1], (owners, LANES)), 0)
    lane = lax.broadcasted_iota(I32, (owners, LANES), 1) * BLOCK
    chunk_vmem[...] = jnp.sum(jnp.where(start + held <= lane, 1, 0), axis=0, keepdims=True)
    carry[...] = start.astype(F32)
    tell = pltpu.make_async_copy(chunk_vmem, chunk_smem, chunk_sem)
    tell.start()

    small[3].wait()
    tile = jnp.maximum(jnp.concatenate([visit[d:d + 1, :] for d in range(depth)], axis=1), 0)
    owner = lax.broadcasted_iota(I32, (1, slots), 1) % owners
    row = owner * (theta // owners) + tile // tiles
    first_phi = (tile % tiles) * PHI_T
    pick = jnp.where(row_hot(row, theta, F32), 1.0, 0.0).astype(BF16)
    spot = lax.broadcasted_iota(I32, (modes, slots), 0)
    n_lines = ring.lines
    mode = (spot % n_lines) * (SQUARE * CORES) + spot // n_lines % SQUARE * CORES + spot // (n_lines * SQUARE)
    angle = ((mode * first_phi) % NPHI).astype(F32) * (2.0 * math.pi / NPHI)
    turn_cos[...] = jnp.cos(angle)
    turn_sin[...] = jnp.sin(angle)
    moved[...] = jnp.zeros_like(moved)
    for copy in small[:2] + small[4:]:
        copy.wait()

    per = blocks // steps

    def rank(i):
        source = jnp.minimum(i, steps - 1)
        masks = [own(source * per + u) for u in range(per)]
        stacked = jnp.concatenate([jnp.where(m, 1.0, 0.0).astype(BF16) for m in masks], axis=0)
        seen = jnp.dot(stacked, rank_mat[...], preferred_element_type=F32)
        base = carry[...]
        for u, mask in enumerate(masks):
            part = seen[u * owners:(u + 1) * owners]
            spots = part[:, :BLOCK] + jnp.concatenate([base] * (BLOCK // LANES), axis=1)
            total = jnp.zeros((8, BLOCK), F32)
            for r in range(0, owners, 8):
                total = jnp.where(mask[r:r + 8], spots[r:r + 8], total)
            dest[pl.ds(i * per + u, 1), :] = jnp.sum(total, axis=0, keepdims=True).astype(I32)
            base = base + part[:, BLOCK:]
        carry[...] = base

    hots = [jnp.ones((BLOCK, BLOCK), BF16), jnp.zeros((BLOCK, BLOCK), BF16)]

    def move(b, to):
        at = block_of(phi, b) * depth + (block_of(slot, b) & (depth - 1))
        mask = row_hot(to >> 8, blocks)
        span = pl.ds(pl.multiple_of(b * BLOCK, BLOCK), BLOCK)
        parts = [at.astype(F32), block_of(psi, b).astype(F32), fraction[0:1, span], fraction[1:2, span]]
        zero = jnp.zeros((blocks, BLOCK), BF16)
        rows = jnp.concatenate(
            [jnp.where(mask, jnp.broadcast_to(p.astype(BF16), (blocks, BLOCK)), zero) for p in parts], axis=0)
        lanes = jnp.where(row_hot(to & 255, BLOCK), *hots)
        hot[span, :] = lanes
        return lax.dot_general(rows, lanes, NT, preferred_element_type=F32)

    size = PHI_T * depth

    def weight(c, s):
        at, along = moved[pl.ds(c, 1), :], moved[pl.ds(2 * blocks + c, 1), :]
        wide_row = lambda w: jnp.broadcast_to(w.astype(BF16), (size, BLOCK))
        both = jnp.where(
            row_hot(at, size), wide_row(1.0 - along),
            jnp.where(row_hot(at + depth, size), wide_row(along), jnp.zeros((size, BLOCK), BF16)))
        weights[pl.ds(pl.multiple_of(c * size, size), size), :] = both
        angle, across = moved[pl.ds(blocks + c, 1), :], moved[pl.ds(3 * blocks + c, 1), :]
        after = jnp.where(angle == NPSI - 1, 0.0, angle + 1.0)
        aims[pl.ds(pl.multiple_of(c * NPSI, NPSI), NPSI), :] = jnp.where(
            row_hot(angle, NPSI), wide_row(1.0 - across),
            jnp.where(row_hot(after, NPSI), wide_row(across), jnp.zeros((NPSI, BLOCK), BF16)))
        return s

    def weigh(j, others):
        part = beam[pl.ds(pl.multiple_of(j * KB, KB), KB), :]
        rows = jnp.concatenate([sky[c:c + 1, :] * part for c in range(2)], axis=0)
        rows = rows.astype(BF16)
        kind = lax.broadcasted_iota(I32, (2 * KB, theta), 0) % KB
        total = jnp.zeros((2 * KB, theta), F32)
        gain = moved[...]
        for kk in range(0, KB, 2):
            pair = jnp.concatenate([wigner[j * KB + kk], wigner[j * KB + kk + 1]], axis=1)
            both = jnp.dot(rows, pair, preferred_element_type=F32)
            for u in range(2):
                total = jnp.where(kind == kk + u, both[:, u * theta:(u + 1) * theta], total)
            for other in others[kk * len(others) // KB:(kk + 2) * len(others) // KB]:
                gain = gain + move(*other)
        moved[...] = gain
        block = total.astype(BF16)
        mine[j] = block
        gathered[j, pl.ds(pl.multiple_of(ring.spot * wide, wide), wide), :] = block

    def synthesize(j, width):
        sides = []
        for w in range(width):
            x = jnp.dot(gathered[j + w], pick, preferred_element_type=F32)
            turned = []
            for m in range(modes):
                re, im = x[m * wide:m * wide + KB], x[m * wide + KB:(m + 1) * wide]
                cm, sm = turn_cos[pl.ds(m, KB, stride=0), :], turn_sin[pl.ds(m, KB, stride=0), :]
                turned.append(jnp.concatenate([cm * re - sm * im, sm * re + cm * im], axis=0).astype(BF16))
            sides.append(jnp.concatenate(turned, axis=0))
        y = jnp.dot(phi_mat[...], jnp.concatenate(sides, axis=1), preferred_element_type=F32)
        for w in range(width):
            for p in range(PHI_T):
                synth[p, pl.ds(pl.multiple_of((j + w) * wide, wide), wide), :] = y[
                    p * wide:(p + 1) * wide, w * slots:(w + 1) * slots].astype(BF16)

    lag = LAG

    def step(i, c):
        load(i).wait()

        @pl.when(i + ahead < steps)
        def _():
            load(i + ahead).start()

        goals = [dest[pl.ds(i * per + u, 1), :] for u in range(per)]
        rank(i + 1)
        weigh(i, [(i * per + u, goal) for u, goal in enumerate(goals)])

        @pl.when(i >= lag[0])
        def _():
            ring.second(i - lag[0])

        @pl.when(i >= lag[1])
        def _():
            ring.third(i - lag[1])

        @pl.when(i < steps - 1)
        def _():
            ring.first(i)

        @pl.when(i == steps - 1)
        def _():
            ring.direct(i)
        return c

    rank(0)
    lax.fori_loop(0, steps, step, 0)
    end = steps - 1
    waits = [(j * 1.5 + 3.75, ring.second, j) for j in range(steps - lag[0], end)]
    waits += [(j * 1.5 + 6.5, ring.third, j) for j in range(steps - lag[1], end)]
    waits.sort(key=lambda w: (w[0], w[2]))
    part = blocks // PARTS
    for n in range(PARTS):
        lax.fori_loop(n * part, (n + 1) * part, weight, 0, unroll=2)
        for _, wait, j in waits[n * len(waits) // PARTS:(n + 1) * len(waits) // PARTS]:
            wait(j)

    def early(j, c):
        ring.last(2 * j)
        ring.last(2 * j + 1)
        synthesize(2 * j, 2)
        return c

    lax.fori_loop(0, end // 2, early, 0)
    if end % 2:
        ring.last(end - 1)
        synthesize(end - 1, 1)
    tell.wait()
    ring.direct_end(end)
    synthesize(end, 1)
    spots = lax.broadcasted_iota(I32, (2 * slots, 2 * slots), 0)
    from_spot = spots // depth % 2 * slots + spots % depth * owners + spots // (2 * depth)
    shuffle = (
        lax.broadcasted_iota(I32, (2 * slots, 2 * slots), 1) == from_spot
    ).astype(F32).astype(BF16)

    def flip(q, c):
        pair = jnp.concatenate([synth[2 * q], synth[2 * q + 1]], axis=1)
        turned = lax.dot_general(shuffle, pair, NT, preferred_element_type=F32)
        rows = 2 * depth
        for o in range(owners):
            lines[pl.ds(pl.multiple_of(o * slots + q * rows, rows), rows), :] = turned[o * rows:(o + 1) * rows]
        return c

    lax.fori_loop(0, PHI_T // 2, flip, 0, unroll=2)

    def cube(p, c):
        part = lines[pl.ds(pl.multiple_of(2 * p * slots, 2 * slots), 2 * slots), :].astype(BF16)
        both = lax.dot_general(psi_mat[...], part, NT, preferred_element_type=F32).astype(BF16)
        for u in range(2):
            table[2 * p + u] = both[:, u * LANES:(u + 1) * LANES]
        return c

    lax.fori_loop(0, owners // 2, cube, 0, unroll=4)
    def meet(c, buffer):
        o = chunk_smem[0, c]
        w = weights[pl.ds(pl.multiple_of(c * size, size), size), :]
        buffer[...] = jnp.dot(table[o], w, preferred_element_type=F32)

    def choose(c, buffer):
        aim = aims[pl.ds(pl.multiple_of(c * NPSI, NPSI), NPSI), :].astype(F32)
        total = jnp.zeros((8, BLOCK), F32)
        for r in range(0, NPSI, 8):
            total = total + buffer[r:r + 8, :] * aim[r:r + 8]
        found[pl.ds(c, 1), :] = jnp.sum(total, axis=0, keepdims=True)

    def pipeline(count, begin, finish, buffers):
        deep = len(buffers) // 2
        for u in range(deep):
            begin(u, buffers[u])

        def both(i, s):
            for side in range(2):
                now = (2 * i + side) * deep
                ahead = jnp.minimum(now + deep, count - deep)
                for u in range(deep):
                    begin(ahead + u, buffers[(1 - side) * deep + u])
                    finish(now + u, buffers[side * deep + u])
            return s

        lax.fori_loop(0, count // (2 * deep), both, 0)

    pipeline(blocks, meet, choose, buffers)
    values = found[...]
    coarse = values.astype(BF16)
    fine = (values - coarse.astype(F32)).astype(BF16)
    found_both[...] = jnp.concatenate([coarse, fine], axis=0)

    def spread(b, buffer):
        lanes = hot[pl.ds(pl.multiple_of(b * BLOCK, BLOCK), BLOCK), :]
        buffer[...] = jnp.dot(found_both[...], lanes, preferred_element_type=F32)

    def settle(b, buffer):
        line = pick_row(dest[pl.ds(b, 1), :] >> 8, buffer.at[0:blocks], buffer.at[blocks:2 * blocks])
        for u in range(BLOCK // LANES):
            out_ref[pl.ds(b * (BLOCK // LANES) + u, 1), :] = line[:, u * LANES:(u + 1) * LANES]

    pipeline(blocks, spread, settle, buffers)
    ring.direct_sent(end)


def run_whole(shards, sky, beam, wigner, visits, point_slot, phi_cell, psi_cell, fraction):
    orders, length, theta = wigner.shape
    owners, depth = visits.shape
    count = point_slot.shape[0]
    blocks = count // BLOCK
    steps, wide = orders // KB, 2 * KB
    slots = owners * depth
    lined = (blocks, BLOCK)
    args = (
        sky, beam, wigner, jnp.transpose(visits), point_slot.reshape(-1, LANES), phi_cell.reshape(-1, LANES),
        psi_cell.reshape(-1, LANES), fraction, phi_matrix(shards), psi_matrix(orders), rank_matrix(),
    )
    return pl.pallas_call(
        functools.partial(whole_kernel, shards, owners, depth),
        out_shape=jax.ShapeDtypeStruct((count // LANES, LANES), F32),
        in_specs=[pl.BlockSpec(memory_space=pl.ANY)] * len(args),
        out_specs=pl.BlockSpec(memory_space=pltpu.VMEM),
        scratch_shapes=[pltpu.VMEM(a.shape, a.dtype) for a in args] + [
            pltpu.VMEM((steps, shards * wide, theta), BF16),
            pltpu.VMEM((steps, wide, theta), BF16),
            pltpu.VMEM((shards, slots), F32),
            pltpu.VMEM((shards, slots), F32),
            pltpu.VMEM((blocks + blocks // steps, BLOCK), I32),
            pltpu.VMEM((owners, LANES), F32),
            pltpu.VMEM((1, LANES), I32),
            pltpu.SMEM((1, LANES), I32),
            pltpu.VMEM((4 * blocks, BLOCK), F32),
            pltpu.VMEM((blocks * BLOCK, BLOCK), BF16),
            pltpu.VMEM((blocks * PHI_T * depth, BLOCK), BF16),
            pltpu.VMEM((blocks * NPSI, BLOCK), BF16),
            pltpu.VMEM((PHI_T, 2 * orders, slots), BF16),
            pltpu.VMEM((PHI_T * slots, 2 * orders), F32),
            pltpu.VMEM((owners, NPSI, LANES), BF16),
            pltpu.VMEM(lined, F32),
            pltpu.VMEM((2 * blocks, BLOCK), BF16),
            *[pltpu.VMEM((max(NPSI, 2 * blocks), BLOCK), F32)] * 8,
            pltpu.SemaphoreType.DMA((steps,)),
            pltpu.SemaphoreType.DMA((len(args) - 1,)),
            pltpu.SemaphoreType.DMA,
            pltpu.SemaphoreType.DMA((steps,)),
            pltpu.SemaphoreType.DMA((3, steps)),
        ],
        compiler_params=pltpu.CompilerParams(collective_id=1, has_side_effects=True, vmem_limit_bytes=67043328),
        name="timeline",
    )(*args).reshape(count)


def interpolate(
    modes,
    orders,
    order_count,
    shard_count,
    coeffs_ref,
    visit_ref,
    phi_table_ref,
    psi_table_ref,
    slot_ref,
    phi_ref,
    psi_ref,
    fraction_ref,
    out_ref,
    picked,
    edge,
    synth,
    wave_a,
    wave_b,
    values_a,
    values_b,
):
    terms = 2 * orders
    high = PHI_T // LOW
    theta = coeffs_ref.shape[1]
    depth, owners = visit_ref.shape
    slots = owners * depth
    blocks = NPHI // (order_count * PHI_T)
    groups = slots // LANES
    listed = jnp.concatenate([visit_ref[d : d + 1, :] for d in range(depth)], axis=1)
    for g in range(groups):
        lanes = slice(g * LANES, (g + 1) * LANES)
        tile = jnp.maximum(listed[:, lanes], 0)
        owner = (lax.broadcasted_iota(jnp.int32, (1, LANES), 1) + g * LANES) % owners
        row = (owner % shard_count) * (theta // shard_count) + tile // blocks
        first_phi = (owner // shard_count) * (NPHI // order_count) + (tile % blocks) * PHI_T
        chosen = (
            lax.broadcasted_iota(jnp.int32, (theta, LANES), 0) == row
        ).astype(jnp.float32).astype(jnp.bfloat16)

        def pick(m, carry):
            rows = pl.ds(pl.multiple_of(m * 4 * terms, 4 * terms), 4 * terms)
            picked[rows, :] = jnp.dot(
                coeffs_ref[rows, :], chosen, preferred_element_type=jnp.float32
            )
            return carry

        lax.fori_loop(0, modes // 4, pick, 0)
        turn = (lax.broadcasted_iota(jnp.int32, (modes, LANES), 0) * first_phi) % NPHI
        angle = turn.astype(jnp.float32) * (2.0 * math.pi / NPHI)
        turn_cos, turn_sin = jnp.cos(angle), jnp.sin(angle)

        def sum_modes(k, carry):
            real = picked[pl.ds(2 * k, modes, stride=terms), :]
            imag = picked[pl.ds(2 * k + 1, modes, stride=terms), :]
            turned = jnp.concatenate(
                [turn_cos * real - turn_sin * imag, turn_sin * real + turn_cos * imag], axis=0
            ).astype(jnp.bfloat16)
            values = jnp.dot(phi_table_ref[...], turned, preferred_element_type=jnp.float32)
            for h in range(high):
                synth[
                    pl.ds(pl.multiple_of(k * 2 * LOW, 2 * LOW), 2 * LOW),
                    h * slots + g * LANES : h * slots + (g + 1) * LANES,
                ] = values[h * 2 * LOW : (h + 1) * 2 * LOW].astype(jnp.bfloat16)
            edge[pl.ds(pl.multiple_of(k * 2 * high, 2 * high), 2 * high), :] = values[
                2 * PHI_T :
            ]
            return carry

        lax.fori_loop(0, orders, sum_modes, 0, unroll=4)
        for part in range(2):
            for h in range(high):
                synth[
                    terms * LOW + part * orders : terms * LOW + (part + 1) * orders,
                    h * slots + g * LANES : h * slots + (g + 1) * LANES,
                ] = edge[pl.ds(part * high + h, orders, stride=2 * high), :].astype(jnp.bfloat16)

    def begin(i, values, wave):
        phi, psi = phi_ref[i], psi_ref[i]
        along_psi = fraction_ref[i][1:2]
        slot = slot_ref[i]
        key = ((phi // LOW) * depth + slot % depth) * owners + slot // depth
        entry = (
            lax.broadcasted_iota(jnp.int32, (high * slots, CHUNK), 0) == key
        ).astype(jnp.float32).astype(jnp.bfloat16)
        at_psi = lax.broadcasted_iota(jnp.int32, (NPSI, CHUNK), 0)
        weight = jnp.where(
            at_psi == psi, 1.0 - along_psi, jnp.where(at_psi == (psi + 1) % NPSI, along_psi, 0.0)
        )
        coarse = weight.astype(jnp.bfloat16)
        fine = (weight - coarse.astype(jnp.float32)).astype(jnp.bfloat16)
        wave[...] = jnp.dot(
            psi_table_ref[...],
            jnp.concatenate([coarse, fine], axis=0),
            preferred_element_type=jnp.float32,
        )
        values[...] = jnp.dot(synth[...], entry, preferred_element_type=jnp.float32)

    def finish(i, values, wave):
        phi = phi_ref[i]
        along_phi = fraction_ref[i][0:1]
        sums = [jnp.zeros((LOW, CHUNK), jnp.float32) for _ in range(4)]
        for k in range(orders):
            for part in range(2):
                at = (2 * k + part) * LOW
                line = part * orders + k
                sums[at // LOW % 4] += values[at : at + LOW, :] * wave[line : line + 1, :]
        inner = (sums[0] + sums[1]) + (sums[2] + sums[3])
        last = jnp.sum(values[terms * LOW :, :] * wave[...], axis=0, keepdims=True)
        low = phi % LOW
        at_low = lax.broadcasted_iota(jnp.int32, (LOW, CHUNK), 0)
        weight_phi = jnp.where(
            at_low == low, 1.0 - along_phi, jnp.where(at_low == low + 1, along_phi, 0.0)
        )
        total = jnp.sum(inner * weight_phi, axis=0, keepdims=True)
        out_ref[i] = total + jnp.where(low == LOW - 1, along_phi, 0.0) * last

    chunks = slot_ref.shape[0]
    begin(0, values_a, wave_a)

    def pair(i, carry):
        begin(2 * i + 1, values_b, wave_b)
        finish(2 * i, values_a, wave_a)
        begin(jnp.minimum(2 * i + 2, chunks - 1), values_a, wave_a)
        finish(2 * i + 1, values_b, wave_b)
        return carry

    lax.fori_loop(0, chunks // 2, pair, 0)


def phi_rows(modes):
    mode = np.arange(modes, dtype=np.int64)[None, :]
    high = PHI_T // LOW
    cos, sin = wave_table(NPHI, np.arange(PHI_T, dtype=np.int64)[:, None], mode)
    real = np.concatenate([cos, -sin], axis=1)
    imag = np.concatenate([sin, cos], axis=1)
    inner = np.stack(
        [real.reshape(high, LOW, 2 * modes), imag.reshape(high, LOW, 2 * modes)], axis=1
    ).reshape(2 * PHI_T, 2 * modes)
    zero = np.zeros((1, 2 * modes), np.float64)
    edge = np.concatenate([real[LOW::LOW], zero, imag[LOW::LOW], zero], axis=0)
    return jnp.asarray(np.concatenate([inner, edge], axis=0), jnp.bfloat16)


def psi_rows(orders):
    order = np.arange(orders, dtype=np.int64)[:, None]
    cos, sin = wave_table(NPSI, np.arange(NPSI, dtype=np.int64)[None, :], order)
    half = np.concatenate([cos, -sin], axis=0)
    return jnp.asarray(np.concatenate([half, half], axis=1), jnp.bfloat16)


def shards(sky_coeffs, beam_coeffs, wigner, visits, point_slot, phi_cell, psi_cell, fraction):
    order_count = lax.axis_size("order")
    shard_count = lax.axis_size("shard")
    local_modes = sky_coeffs.shape[0]
    local_orders = beam_coeffs.shape[0]
    theta_count = wigner.shape[3]
    orders = local_orders * order_count
    modes = local_modes * shard_count
    lines = shard_count // (SQUARE * CORES)
    if grouped(lines, order_count, modes, orders, visits.shape[1:], point_slot.shape[0], theta_count):
        return run_whole(
            shard_count, sky_coeffs[0], beam_coeffs, wigner[0], visits[0], point_slot, phi_cell, psi_cell, fraction
        )
    weighted = (sky_coeffs[:, None, :, :] * beam_coeffs[None, :, None, :]).astype(jnp.bfloat16)
    coeffs = jnp.einsum("mkcl,mklt->mkct", weighted, wigner, preferred_element_type=jnp.float32)
    coeffs = coeffs.astype(jnp.bfloat16).reshape(local_modes * local_orders * 2, theta_count)
    coeffs = pl.pallas_call(
        functools.partial(gather_blocks, shard_count // (SQUARE * CORES)),
        out_shape=jax.ShapeDtypeStruct((shard_count * coeffs.shape[0], theta_count), jnp.bfloat16),
        in_specs=[pl.BlockSpec(memory_space=pltpu.VMEM)],
        out_specs=pl.BlockSpec(memory_space=pltpu.VMEM),
        scratch_shapes=[
            pltpu.SemaphoreType.DMA((shard_count - 1,)),
            pltpu.SemaphoreType.DMA((shard_count,)),
        ],
        compiler_params=pltpu.CompilerParams(collective_id=0, has_side_effects=True),
    )(coeffs)
    if order_count > 1:
        coeffs = coeffs.reshape(modes, local_orders * 2, theta_count)
        coeffs = lax.all_gather(coeffs, "order", axis=1, tiled=True)
        coeffs = coeffs.reshape(modes * orders * 2, theta_count)

    slots = visits.shape[1] * visits.shape[2]
    count = point_slot.shape[0]
    chunks = count // CHUNK
    lined = (chunks, 1, CHUNK)
    pairs = jnp.transpose(fraction.reshape(2, chunks, CHUNK), (1, 0, 2))
    high = PHI_T // LOW
    timeline = pl.pallas_call(
        functools.partial(
            interpolate, modes, orders, order_count, shard_count
        ),
        out_shape=jax.ShapeDtypeStruct(lined, jnp.float32),
        in_specs=[pl.BlockSpec(memory_space=pltpu.VMEM)] * 8,
        out_specs=pl.BlockSpec(memory_space=pltpu.VMEM),
        scratch_shapes=[
            pltpu.VMEM((modes * orders * 2, LANES), jnp.float32),
            pltpu.VMEM((orders * 2 * high, LANES), jnp.float32),
            pltpu.VMEM((orders * 2 * (LOW + 1), high * slots), jnp.bfloat16),
            pltpu.VMEM((orders * 2, CHUNK), jnp.float32),
            pltpu.VMEM((orders * 2, CHUNK), jnp.float32),
            pltpu.VMEM((orders * 2 * (LOW + 1), CHUNK), jnp.float32),
            pltpu.VMEM((orders * 2 * (LOW + 1), CHUNK), jnp.float32),
        ],
    )(
        coeffs,
        jnp.transpose(visits[0]),
        phi_rows(modes),
        psi_rows(orders),
        point_slot.reshape(lined),
        phi_cell.reshape(lined),
        psi_cell.reshape(lined),
        pairs,
    )
    return timeline.reshape(count)


def solution(mesh):
    placed = (
        P("shard", None, None),
        P("order", None),
        P("shard", "order", None, None),
        P(("order", "shard"), None, None),
        P(("order", "shard")),
        P(("order", "shard")),
        P(("order", "shard")),
        P(None, ("order", "shard")),
    )
    return jax.shard_map(
        shards, mesh=mesh, in_specs=placed, out_specs=P(("order", "shard")), check_vma=False
    )
```

```python
import functools
import math

import jax
import jax.numpy as jnp
import numpy as np
from jax import lax
from jax.experimental import pallas as pl
from jax.experimental.pallas import tpu as pltpu
from jax.sharding import PartitionSpec as P

NPHI = 4096
NPSI = 128
PHI_T = 32
LOW = 8
LANES = 128
CHUNK = 256
KB = 8
BLOCK = 256
F32, BF16, I32 = jnp.float32, jnp.bfloat16, jnp.int32


SQUARE = 4
CORES = 2


def gather_blocks(lines, block_ref, out_ref, send_sem, recv_sem):
    me = lax.axis_index("shard")
    core = me % CORES
    square = me // CORES % SQUARE
    line = me // (CORES * SQUARE)
    depth = block_ref.shape[0]

    def index(at_line, at_square, at_core):
        return (at_line * SQUARE + at_square) * CORES + at_core

    along = [(line + d) % lines for d in range(1, lines)]
    if lines == 4:
        half = line // 2
        along = [line + 1 - 2 * (line % 2), 2 - half, 3 - 3 * half]
    across = [(square + d) % SQUARE for d in range(1, SQUARE)]
    other = (core + 1) % CORES
    line_peers = [index(a, square, core) for a in along]
    square_peers = [index(line, b, core) for b in across]
    twin = index(line, square, other)
    barrier = pltpu.get_barrier_semaphore()
    peers = line_peers + square_peers + [twin]
    for peer in peers:
        pl.semaphore_signal(
            barrier, inc=1, device_id={"shard": peer}, device_id_type=pl.DeviceIdType.MESH
        )
    pl.semaphore_wait(barrier, len(peers))

    started = []

    def place(owner):
        return out_ref.at[pl.ds(pl.multiple_of(owner * depth, depth), depth), :]

    def send(source, owner, peer):
        copy = pltpu.make_async_remote_copy(
            src_ref=source,
            dst_ref=place(owner),
            send_sem=send_sem.at[len(started)],
            recv_sem=recv_sem.at[owner],
            device_id={"shard": peer},
            device_id_type=pl.DeviceIdType.MESH,
        )
        copy.start()
        started.append(copy)

    def arrive(owner):
        pltpu.make_async_remote_copy(
            src_ref=place(owner),
            dst_ref=place(owner),
            send_sem=send_sem.at[0],
            recv_sem=recv_sem.at[owner],
            device_id={"shard": twin},
            device_id_type=pl.DeviceIdType.MESH,
        ).wait_recv()

    for peer in line_peers[::-1] + square_peers + [twin]:
        send(block_ref, me, peer)
    out_ref[pl.ds(pl.multiple_of(me * depth, depth), depth), :] = block_ref[...]
    for owner in line_peers:
        arrive(owner)
        for peer in square_peers + [twin]:
            send(place(owner), owner, peer)
    for a in [line] + along:
        for b in across:
            owner = index(a, b, core)
            arrive(owner)
            send(place(owner), owner, twin)
    for a in [line] + along:
        for b in [square] + across:
            arrive(index(a, b, other))
    for copy in started:
        copy.wait_send()


def wave_table(count, grid, mode):
    phase = 2.0 * math.pi * ((grid * mode) % count) / count
    return np.cos(phase), np.sin(phase)


INSIDE = True
EARLY = True
FINE = True
PARTS = 4
AHEAD = 2
LAG = (3, 5)
NT = (((1,), (1,)), ((), ()))


def grouped(lines, order_count, modes, orders, visits, count, theta):
    owners, depth = visits
    return (
        lines > 1
        and order_count == 1
        and modes == owners
        and orders % KB == 0
        and 2 * orders == theta == owners * depth == PHI_T * depth == NPSI == LANES
        and count % (2 * owners * BLOCK) == 0
        and count == orders * BLOCK
    )


def row_hot(index, size, dtype=BF16):
    n = index.shape[1]
    rows = lax.broadcasted_iota(I32, (size, n), 0)
    if dtype == BF16:
        return rows.astype(F32).astype(BF16) == jnp.broadcast_to(index.astype(F32).astype(BF16), (size, n))
    return rows == index


def pick_row(index, *values):
    size, n = values[0].shape
    totals = [jnp.zeros((8, n), F32) for _ in values]
    index = jnp.broadcast_to(index, (8, n)) - lax.broadcasted_iota(I32, (8, n), 0)
    for r in range(0, size, 8):
        mask = index == r
        totals = [jnp.where(mask, v[r:r + 8], t) for v, t in zip(values, totals)]
    return jnp.sum(functools.reduce(jnp.add, totals), axis=0, keepdims=True)


def block_of(ref, b):
    per = BLOCK // LANES
    return jnp.concatenate([ref[pl.ds(b * per + u, 1), :] for u in range(per)], axis=1)


def mode_order(modes):
    lines = modes // (SQUARE * CORES)
    place = np.arange(modes)
    return (place % lines) * SQUARE * CORES + place // lines % SQUARE * CORES + place // (lines * SQUARE)


def phi_matrix(modes):
    cos, sin = wave_table(NPHI, np.arange(PHI_T)[:, None], mode_order(modes)[None, :])
    core = np.stack([np.stack([cos, -sin], -1), np.stack([sin, cos], -1)], 1)
    full = np.einsum("pamc,kj->pakmcj", core, np.eye(KB))
    return jnp.asarray(full.reshape(PHI_T * 2 * KB, modes * 2 * KB), BF16)


def psi_matrix(orders):
    cos, sin = wave_table(NPSI, np.arange(NPSI)[:, None], np.arange(orders)[None, :])
    pair = np.stack([cos.reshape(NPSI, -1, KB), -sin.reshape(NPSI, -1, KB)], 2)
    return jnp.asarray(pair.reshape(NPSI, 2 * orders), BF16)


def rank_matrix():
    i = np.arange(BLOCK)
    upper = (i[:, None] < i[None, :]).astype(np.float32)
    return jnp.asarray(np.concatenate([upper, np.ones((BLOCK, LANES), np.float32)], 1), BF16)


class Ring:
    def __init__(self, shards, mine, out, send_sem, recv_sem):
        lines = shards // (SQUARE * CORES)
        me = lax.axis_index("shard")
        core, square, line = me % CORES, me // CORES % SQUARE, me // (CORES * SQUARE)
        index = lambda a, b, c: (a * SQUARE + b) * CORES + c
        along = [(line + d) % lines for d in range(1, lines)]
        across = [(square + d) % SQUARE for d in range(1, SQUARE)]
        other = (core + 1) % CORES
        self.shards, self.lines = shards, lines
        self.line_peers = [index(a, square, core) for a in along]
        self.square_peers = [index(line, b, core) for b in across]
        self.twin = index(line, square, other)
        self.all_peers = [
            index(a, b, c) for a in along[::-1] + [line] for b in across[::-1] + [square] for c in (other, core)
        ][:-1]
        self.mine, self.out, self.send_sem, self.recv_sem = mine, out, send_sem, recv_sem
        self.wide = mine.shape[1]
        self.column = core * SQUARE + square
        self.columns = [core * SQUARE + b for b in across]
        self.spot = self.column * lines + line

    def hail(self):
        barrier = pltpu.get_barrier_semaphore()
        for peer in self.all_peers:
            pl.semaphore_signal(barrier, inc=1, device_id={"shard": peer}, device_id_type=pl.DeviceIdType.MESH)

    def meet(self):
        pl.semaphore_wait(pltpu.get_barrier_semaphore(), len(self.all_peers))

    def place(self, j, first, count):
        return self.out.at[j, pl.ds(pl.multiple_of(first * self.wide, self.wide), count * self.wide), :]

    def copy(self, source, target, j, peer, kind):
        return pltpu.make_async_remote_copy(
            src_ref=source,
            dst_ref=target,
            send_sem=self.send_sem.at[j],
            recv_sem=self.recv_sem.at[kind, j],
            device_id={"shard": peer},
            device_id_type=pl.DeviceIdType.MESH,
        )

    def arrive(self, j, kind, blocks):
        span = self.place(j, 0, blocks)
        self.copy(span, span, j, self.twin, kind).wait_recv()

    def sent(self, j, blocks):
        span = self.place(j, 0, blocks)
        self.copy(span, span, j, self.twin, 0).wait_send()

    def first(self, j):
        for peer in self.line_peers:
            self.copy(self.mine.at[j], self.place(j, self.spot, 1), j, peer, 0).start()

    def second(self, j):
        self.arrive(j, 0, self.lines - 1)
        span = self.place(j, self.column * self.lines, self.lines)
        for peer in self.square_peers:
            self.copy(span, span, j, peer, 1).start()
        self.copy(span, span, j, self.twin, 2).start()

    def third(self, j):
        self.arrive(j, 1, (SQUARE - 1) * self.lines)
        for column in self.columns:
            span = self.place(j, column * self.lines, self.lines)
            self.copy(span, span, j, self.twin, 2).start()

    def last(self, j):
        self.arrive(j, 2, SQUARE * self.lines)
        self.sent(j, self.lines - 1)
        self.sent(j, (2 * SQUARE - 1) * self.lines)

    def direct(self, j):
        for peer in self.all_peers:
            self.copy(self.mine.at[j], self.place(j, self.spot, 1), j, peer, 0).start()

    def direct_end(self, j):
        self.arrive(j, 0, self.shards - 1)

    def direct_sent(self, j):
        self.sent(j, self.shards - 1)


def whole_kernel(
    shards, owners, depth,
    sky_hbm, beam_hbm, wigner_hbm, visit_hbm, slot_hbm, phi_hbm, psi_hbm, fraction_hbm, phi_mat_hbm, psi_mat_hbm, rank_hbm,
    out_ref,
    sky, beam, wigner, visit, slot, phi, psi, fraction, phi_mat, psi_mat, rank_mat,
    gathered, mine, turn_cos, turn_sin, dest, carry, chunk_vmem, chunk_smem, moved, hot, weights, aims, synth, lines, table, found, found_both, *rest,
):
    *buffers, load_sem, small_sem, chunk_sem, send_sem, recv_sem = rest
    steps, wide = mine.shape[0], mine.shape[1]
    modes = shards
    theta = wigner.shape[2]
    slots = owners * depth
    blocks = found.shape[0]
    tiles = NPHI // PHI_T
    ring = Ring(shards, mine, gathered, send_sem, recv_sem)

    small = [
        (sky_hbm, sky), (beam_hbm, beam), (slot_hbm, slot), (visit_hbm, visit), (rank_hbm, rank_mat),
        (phi_hbm, phi), (psi_hbm, psi), (fraction_hbm, fraction), (phi_mat_hbm, phi_mat), (psi_mat_hbm, psi_mat),
    ]
    small = [pltpu.make_async_copy(s, d, small_sem.at[n]) for n, (s, d) in enumerate(small)]

    def load(j):
        rows = pl.ds(j * KB, KB)
        return pltpu.make_async_copy(wigner_hbm.at[rows], wigner.at[rows], load_sem.at[j])

    for copy in small[:4]:
        copy.start()
    load(0).start()
    for copy in small[4:]:
        copy.start()
    ahead = AHEAD
    if EARLY:
        for j in range(1, ahead):
            load(j).start()
    ring.hail()

    small[2].wait()

    def own(b):
        owner = block_of(slot, b) >> int(math.log2(depth))
        return lax.broadcasted_iota(I32, (owners, BLOCK), 0) == owner

    def count(b, total):
        return total + jnp.where(own(b), 1, 0)

    total = lax.fori_loop(0, blocks, count, jnp.zeros((owners, BLOCK), I32), unroll=8)
    held = jnp.broadcast_to(jnp.sum(total, axis=1, keepdims=True), (owners, LANES))
    place = lax.broadcasted_iota(I32, (owners, LANES), 0)
    start = jnp.zeros((owners, LANES), I32)
    for o in range(owners - 1):
        start = start + jnp.where(place > o, jnp.broadcast_to(held[o:o + 1], (owners, LANES)), 0)
    lane = lax.broadcasted_iota(I32, (owners, LANES), 1) * BLOCK
    chunk_vmem[...] = jnp.sum(jnp.where(start + held <= lane, 1, 0), axis=0, keepdims=True)
    carry[...] = start.astype(F32)
    tell = pltpu.make_async_copy(chunk_vmem, chunk_smem, chunk_sem)
    tell.start()

    small[3].wait()
    tile = jnp.maximum(jnp.concatenate([visit[d:d + 1, :] for d in range(depth)], axis=1), 0)
    owner = lax.broadcasted_iota(I32, (1, slots), 1) % owners
    row = owner * (theta // owners) + tile // tiles
    first_phi = (tile % tiles) * PHI_T
    pick = jnp.where(row_hot(row, theta, F32), 1.0, 0.0).astype(BF16)
    spot = lax.broadcasted_iota(I32, (modes, slots), 0)
    n_lines = ring.lines
    mode = (spot % n_lines) * (SQUARE * CORES) + spot // n_lines % SQUARE * CORES + spot // (n_lines * SQUARE)
    angle = ((mode * first_phi) % NPHI).astype(F32) * (2.0 * math.pi / NPHI)
    turn_cos[...] = jnp.cos(angle)
    turn_sin[...] = jnp.sin(angle)
    moved[...] = jnp.zeros_like(moved)
    for copy in small[:2] + small[4:]:
        copy.wait()

    per = blocks // steps

    def rank(i):
        source = jnp.minimum(i, steps - 1)
        masks = [own(source * per + u) for u in range(per)]
        stacked = jnp.concatenate([jnp.where(m, 1.0, 0.0).astype(BF16) for m in masks], axis=0)
        seen = jnp.dot(stacked, rank_mat[...], preferred_element_type=F32)
        base = carry[...]
        for u, mask in enumerate(masks):
            part = seen[u * owners:(u + 1) * owners]
            spots = part[:, :BLOCK] + jnp.concatenate([base] * (BLOCK // LANES), axis=1)
            total = jnp.zeros((8, BLOCK), F32)
            for r in range(0, owners, 8):
                total = jnp.where(mask[r:r + 8], spots[r:r + 8], total)
            dest[pl.ds(i * per + u, 1), :] = jnp.sum(total, axis=0, keepdims=True).astype(I32)
            base = base + part[:, BLOCK:]
        carry[...] = base

    hots = [jnp.ones((BLOCK, BLOCK), BF16), jnp.zeros((BLOCK, BLOCK), BF16)]

    def move(b, to):
        at = block_of(phi, b) * depth + (block_of(slot, b) & (depth - 1))
        mask = row_hot(to >> 8, blocks)
        span = pl.ds(pl.multiple_of(b * BLOCK, BLOCK), BLOCK)
        parts = [at.astype(F32), block_of(psi, b).astype(F32), fraction[0:1, span], fraction[1:2, span]]
        zero = jnp.zeros((blocks, BLOCK), BF16)
        rows = jnp.concatenate(
            [jnp.where(mask, jnp.broadcast_to(p.astype(BF16), (blocks, BLOCK)), zero) for p in parts], axis=0)
        lanes = jnp.where(row_hot(to & 255, BLOCK), *hots)
        hot[span, :] = lanes
        return lax.dot_general(rows, lanes, NT, preferred_element_type=F32)

    size = PHI_T * depth

    def weight(c, s):
        at, along = moved[pl.ds(c, 1), :], moved[pl.ds(2 * blocks + c, 1), :]
        wide_row = lambda w: jnp.broadcast_to(w.astype(BF16), (size, BLOCK))
        both = jnp.where(
            row_hot(at, size), wide_row(1.0 - along),
            jnp.where(row_hot(at + depth, size), wide_row(along), jnp.zeros((size, BLOCK), BF16)))
        weights[pl.ds(pl.multiple_of(c * size, size), size), :] = both
        angle, across = moved[pl.ds(blocks + c, 1), :], moved[pl.ds(3 * blocks + c, 1), :]
        after = jnp.where(angle == NPSI - 1, 0.0, angle + 1.0)
        aims[pl.ds(pl.multiple_of(c * NPSI, NPSI), NPSI), :] = jnp.where(
            row_hot(angle, NPSI), wide_row(1.0 - across),
            jnp.where(row_hot(after, NPSI), wide_row(across), jnp.zeros((NPSI, BLOCK), BF16)))
        return s

    def weigh(j, others):
        part = beam[pl.ds(pl.multiple_of(j * KB, KB), KB), :]
        rows = jnp.concatenate([sky[c:c + 1, :] * part for c in range(2)], axis=0)
        rows = rows.astype(BF16)
        kind = lax.broadcasted_iota(I32, (2 * KB, theta), 0) % KB
        total = jnp.zeros((2 * KB, theta), F32)
        gain = moved[...]
        for kk in range(0, KB, 2):
            pair = jnp.concatenate([wigner[j * KB + kk], wigner[j * KB + kk + 1]], axis=1)
            both = jnp.dot(rows, pair, preferred_element_type=F32)
            for u in range(2):
                total = jnp.where(kind == kk + u, both[:, u * theta:(u + 1) * theta], total)
            for other in others[kk * len(others) // KB:(kk + 2) * len(others) // KB]:
                gain = gain + move(*other)
        moved[...] = gain
        block = total.astype(BF16)
        mine[j] = block
        gathered[j, pl.ds(pl.multiple_of(ring.spot * wide, wide), wide), :] = block

    def synthesize(j, width):
        sides = []
        for w in range(width):
            x = jnp.dot(gathered[j + w], pick, preferred_element_type=F32)
            turned = []
            for m in range(modes):
                re, im = x[m * wide:m * wide + KB], x[m * wide + KB:(m + 1) * wide]
                cm, sm = turn_cos[pl.ds(m, KB, stride=0), :], turn_sin[pl.ds(m, KB, stride=0), :]
                turned.append(jnp.concatenate([cm * re - sm * im, sm * re + cm * im], axis=0).astype(BF16))
            sides.append(jnp.concatenate(turned, axis=0))
        y = jnp.dot(phi_mat[...], jnp.concatenate(sides, axis=1), preferred_element_type=F32)
        for w in range(width):
            for p in range(PHI_T):
                synth[p, pl.ds(pl.multiple_of((j + w) * wide, wide), wide), :] = y[
                    p * wide:(p + 1) * wide, w * slots:(w + 1) * slots].astype(BF16)

    lag = LAG

    def step(i, c):
        load(i).wait()

        @pl.when(i + ahead < steps)
        def _():
            load(i + ahead).start()

        goals = [dest[pl.ds(i * per + u, 1), :] for u in range(per)]
        rank(i + 1)
        weigh(i, [(i * per + u, goal) for u, goal in enumerate(goals)])

        if INSIDE:
            @pl.when(i == 0)
            def _():
                ring.meet()

        @pl.when(i >= lag[0])
        def _():
            ring.second(i - lag[0])

        @pl.when(i >= lag[1])
        def _():
            ring.third(i - lag[1])

        @pl.when(i < steps - 1)
        def _():
            ring.first(i)

        @pl.when(i == steps - 1)
        def _():
            ring.direct(i)
        return c

    if not EARLY:
        for j in range(1, ahead):
            load(j).start()
    rank(0)
    if not INSIDE:
        ring.meet()
    lax.fori_loop(0, steps, step, 0)
    end = steps - 1
    waits = [(j * 1.5 + 3.75, ring.second, j) for j in range(steps - lag[0], end)]
    waits += [(j * 1.5 + 6.5, ring.third, j) for j in range(steps - lag[1], end)]
    waits.sort(key=lambda w: (w[0], w[2]))
    part = blocks // PARTS
    for n in range(PARTS):
        lax.fori_loop(n * part, (n + 1) * part, weight, 0, unroll=2)
        for _, wait, j in waits[n * len(waits) // PARTS:(n + 1) * len(waits) // PARTS]:
            wait(j)

    def early(j, c):
        ring.last(2 * j)
        ring.last(2 * j + 1)
        synthesize(2 * j, 2)
        return c

    lax.fori_loop(0, end // 2, early, 0)
    if end % 2:
        ring.last(end - 1)
        synthesize(end - 1, 1)
    tell.wait()
    ring.direct_end(end)
    synthesize(end, 1)
    spots = lax.broadcasted_iota(I32, (2 * slots, 2 * slots), 0)
    from_spot = spots // depth % 2 * slots + spots % depth * owners + spots // (2 * depth)
    shuffle = (
        lax.broadcasted_iota(I32, (2 * slots, 2 * slots), 1) == from_spot
    ).astype(F32).astype(BF16)

    def flip(q, c):
        pairs = [
            jnp.concatenate([synth[4 * q + 2 * u], synth[4 * q + 2 * u + 1]], axis=1) for u in range(2)
        ]
        turned = lax.dot_general(shuffle, jnp.concatenate(pairs, axis=0), NT, preferred_element_type=F32)
        rows = 2 * depth
        for o in range(owners):
            for u in range(2):
                lines[pl.ds(pl.multiple_of(o * slots + (2 * q + u) * rows, rows), rows), :] = turned[
                    o * rows:(o + 1) * rows, u * LANES:(u + 1) * LANES]
        return c

    lax.fori_loop(0, PHI_T // 4, flip, 0, unroll=2)

    def cube(p, c):
        part = lines[pl.ds(pl.multiple_of(2 * p * slots, 2 * slots), 2 * slots), :].astype(BF16)
        both = lax.dot_general(psi_mat[...], part, NT, preferred_element_type=F32).astype(BF16)
        for u in range(2):
            table[2 * p + u] = both[:, u * LANES:(u + 1) * LANES]
        return c

    lax.fori_loop(0, owners // 2, cube, 0, unroll=8)
    def meet(c, buffer):
        o = chunk_smem[0, c]
        w = weights[pl.ds(pl.multiple_of(c * size, size), size), :]
        buffer[...] = jnp.dot(table[o], w, preferred_element_type=F32)

    def choose(c, buffer):
        aim = aims[pl.ds(pl.multiple_of(c * NPSI, NPSI), NPSI), :].astype(F32)
        total = jnp.zeros((8, BLOCK), F32)
        for r in range(0, NPSI, 8):
            total = total + buffer[r:r + 8, :] * aim[r:r + 8]
        found[pl.ds(c, 1), :] = jnp.sum(total, axis=0, keepdims=True)

    def pipeline(count, begin, finish, buffers):
        deep = len(buffers) // 2
        for u in range(deep):
            begin(u, buffers[u])

        def both(i, s):
            for side in range(2):
                now = (2 * i + side) * deep
                ahead = jnp.minimum(now + deep, count - deep)
                for u in range(deep):
                    begin(ahead + u, buffers[(1 - side) * deep + u])
                    finish(now + u, buffers[side * deep + u])
            return s

        lax.fori_loop(0, count // (2 * deep), both, 0)

    pipeline(blocks, meet, choose, buffers)
    values = found[...]
    coarse = values.astype(BF16)
    if FINE:
        found_both[...] = jnp.concatenate([coarse, (values - coarse.astype(F32)).astype(BF16)], axis=0)
    else:
        found_both[0:blocks] = coarse

    def spread(b, buffer):
        lanes = hot[pl.ds(pl.multiple_of(b * BLOCK, BLOCK), BLOCK), :]
        height = 2 * blocks if FINE else blocks
        buffer[0:height] = jnp.dot(found_both[0:height], lanes, preferred_element_type=F32)

    def settle(b, buffer):
        parts = [buffer.at[0:blocks], buffer.at[blocks:2 * blocks]] if FINE else [buffer.at[0:blocks]]
        line = pick_row(dest[pl.ds(b, 1), :] >> 8, *parts)
        for u in range(BLOCK // LANES):
            out_ref[pl.ds(b * (BLOCK // LANES) + u, 1), :] = line[:, u * LANES:(u + 1) * LANES]

    pipeline(blocks, spread, settle, buffers)
    ring.direct_sent(end)


def run_whole(shards, sky, beam, wigner, visits, point_slot, phi_cell, psi_cell, fraction):
    orders, length, theta = wigner.shape
    owners, depth = visits.shape
    count = point_slot.shape[0]
    blocks = count // BLOCK
    steps, wide = orders // KB, 2 * KB
    slots = owners * depth
    lined = (blocks, BLOCK)
    args = (
        sky, beam, wigner, jnp.transpose(visits), point_slot.reshape(-1, LANES), phi_cell.reshape(-1, LANES),
        psi_cell.reshape(-1, LANES), fraction, phi_matrix(shards), psi_matrix(orders), rank_matrix(),
    )
    return pl.pallas_call(
        functools.partial(whole_kernel, shards, owners, depth),
        out_shape=jax.ShapeDtypeStruct((count // LANES, LANES), F32),
        in_specs=[pl.BlockSpec(memory_space=pl.ANY)] * len(args),
        out_specs=pl.BlockSpec(memory_space=pltpu.VMEM),
        scratch_shapes=[pltpu.VMEM(a.shape, a.dtype) for a in args] + [
            pltpu.VMEM((steps, shards * wide, theta), BF16),
            pltpu.VMEM((steps, wide, theta), BF16),
            pltpu.VMEM((shards, slots), F32),
            pltpu.VMEM((shards, slots), F32),
            pltpu.VMEM((blocks + blocks // steps, BLOCK), I32),
            pltpu.VMEM((owners, LANES), F32),
            pltpu.VMEM((1, LANES), I32),
            pltpu.SMEM((1, LANES), I32),
            pltpu.VMEM((4 * blocks, BLOCK), F32),
            pltpu.VMEM((blocks * BLOCK, BLOCK), BF16),
            pltpu.VMEM((blocks * PHI_T * depth, BLOCK), BF16),
            pltpu.VMEM((blocks * NPSI, BLOCK), BF16),
            pltpu.VMEM((PHI_T, 2 * orders, slots), BF16),
            pltpu.VMEM((PHI_T * slots, 2 * orders), F32),
            pltpu.VMEM((owners, NPSI, LANES), BF16),
            pltpu.VMEM(lined, F32),
            pltpu.VMEM((2 * blocks, BLOCK), BF16),
            *[pltpu.VMEM((max(NPSI, 2 * blocks), BLOCK), F32)] * 8,
            pltpu.SemaphoreType.DMA((steps,)),
            pltpu.SemaphoreType.DMA((len(args) - 1,)),
            pltpu.SemaphoreType.DMA,
            pltpu.SemaphoreType.DMA((steps,)),
            pltpu.SemaphoreType.DMA((3, steps)),
        ],
        compiler_params=pltpu.CompilerParams(collective_id=1, has_side_effects=True, vmem_limit_bytes=67043328),
        name="timeline",
    )(*args).reshape(count)


def interpolate(
    modes,
    orders,
    order_count,
    shard_count,
    coeffs_ref,
    visit_ref,
    phi_table_ref,
    psi_table_ref,
    slot_ref,
    phi_ref,
    psi_ref,
    fraction_ref,
    out_ref,
    picked,
    edge,
    synth,
    wave_a,
    wave_b,
    values_a,
    values_b,
):
    terms = 2 * orders
    high = PHI_T // LOW
    theta = coeffs_ref.shape[1]
    depth, owners = visit_ref.shape
    slots = owners * depth
    blocks = NPHI // (order_count * PHI_T)
    groups = slots // LANES
    listed = jnp.concatenate([visit_ref[d : d + 1, :] for d in range(depth)], axis=1)
    for g in range(groups):
        lanes = slice(g * LANES, (g + 1) * LANES)
        tile = jnp.maximum(listed[:, lanes], 0)
        owner = (lax.broadcasted_iota(jnp.int32, (1, LANES), 1) + g * LANES) % owners
        row = (owner % shard_count) * (theta // shard_count) + tile // blocks
        first_phi = (owner // shard_count) * (NPHI // order_count) + (tile % blocks) * PHI_T
        chosen = (
            lax.broadcasted_iota(jnp.int32, (theta, LANES), 0) == row
        ).astype(jnp.float32).astype(jnp.bfloat16)

        def pick(m, carry):
            rows = pl.ds(pl.multiple_of(m * 4 * terms, 4 * terms), 4 * terms)
            picked[rows, :] = jnp.dot(
                coeffs_ref[rows, :], chosen, preferred_element_type=jnp.float32
            )
            return carry

        lax.fori_loop(0, modes // 4, pick, 0)
        turn = (lax.broadcasted_iota(jnp.int32, (modes, LANES), 0) * first_phi) % NPHI
        angle = turn.astype(jnp.float32) * (2.0 * math.pi / NPHI)
        turn_cos, turn_sin = jnp.cos(angle), jnp.sin(angle)

        def sum_modes(k, carry):
            real = picked[pl.ds(2 * k, modes, stride=terms), :]
            imag = picked[pl.ds(2 * k + 1, modes, stride=terms), :]
            turned = jnp.concatenate(
                [turn_cos * real - turn_sin * imag, turn_sin * real + turn_cos * imag], axis=0
            ).astype(jnp.bfloat16)
            values = jnp.dot(phi_table_ref[...], turned, preferred_element_type=jnp.float32)
            for h in range(high):
                synth[
                    pl.ds(pl.multiple_of(k * 2 * LOW, 2 * LOW), 2 * LOW),
                    h * slots + g * LANES : h * slots + (g + 1) * LANES,
                ] = values[h * 2 * LOW : (h + 1) * 2 * LOW].astype(jnp.bfloat16)
            edge[pl.ds(pl.multiple_of(k * 2 * high, 2 * high), 2 * high), :] = values[
                2 * PHI_T :
            ]
            return carry

        lax.fori_loop(0, orders, sum_modes, 0, unroll=4)
        for part in range(2):
            for h in range(high):
                synth[
                    terms * LOW + part * orders : terms * LOW + (part + 1) * orders,
                    h * slots + g * LANES : h * slots + (g + 1) * LANES,
                ] = edge[pl.ds(part * high + h, orders, stride=2 * high), :].astype(jnp.bfloat16)

    def begin(i, values, wave):
        phi, psi = phi_ref[i], psi_ref[i]
        along_psi = fraction_ref[i][1:2]
        slot = slot_ref[i]
        key = ((phi // LOW) * depth + slot % depth) * owners + slot // depth
        entry = (
            lax.broadcasted_iota(jnp.int32, (high * slots, CHUNK), 0) == key
        ).astype(jnp.float32).astype(jnp.bfloat16)
        at_psi = lax.broadcasted_iota(jnp.int32, (NPSI, CHUNK), 0)
        weight = jnp.where(
            at_psi == psi, 1.0 - along_psi, jnp.where(at_psi == (psi + 1) % NPSI, along_psi, 0.0)
        )
        coarse = weight.astype(jnp.bfloat16)
        fine = (weight - coarse.astype(jnp.float32)).astype(jnp.bfloat16)
        wave[...] = jnp.dot(
            psi_table_ref[...],
            jnp.concatenate([coarse, fine], axis=0),
            preferred_element_type=jnp.float32,
        )
        values[...] = jnp.dot(synth[...], entry, preferred_element_type=jnp.float32)

    def finish(i, values, wave):
        phi = phi_ref[i]
        along_phi = fraction_ref[i][0:1]
        sums = [jnp.zeros((LOW, CHUNK), jnp.float32) for _ in range(4)]
        for k in range(orders):
            for part in range(2):
                at = (2 * k + part) * LOW
                line = part * orders + k
                sums[at // LOW % 4] += values[at : at + LOW, :] * wave[line : line + 1, :]
        inner = (sums[0] + sums[1]) + (sums[2] + sums[3])
        last = jnp.sum(values[terms * LOW :, :] * wave[...], axis=0, keepdims=True)
        low = phi % LOW
        at_low = lax.broadcasted_iota(jnp.int32, (LOW, CHUNK), 0)
        weight_phi = jnp.where(
            at_low == low, 1.0 - along_phi, jnp.where(at_low == low + 1, along_phi, 0.0)
        )
        total = jnp.sum(inner * weight_phi, axis=0, keepdims=True)
        out_ref[i] = total + jnp.where(low == LOW - 1, along_phi, 0.0) * last

    chunks = slot_ref.shape[0]
    begin(0, values_a, wave_a)

    def pair(i, carry):
        begin(2 * i + 1, values_b, wave_b)
        finish(2 * i, values_a, wave_a)
        begin(jnp.minimum(2 * i + 2, chunks - 1), values_a, wave_a)
        finish(2 * i + 1, values_b, wave_b)
        return carry

    lax.fori_loop(0, chunks // 2, pair, 0)


def phi_rows(modes):
    mode = np.arange(modes, dtype=np.int64)[None, :]
    high = PHI_T // LOW
    cos, sin = wave_table(NPHI, np.arange(PHI_T, dtype=np.int64)[:, None], mode)
    real = np.concatenate([cos, -sin], axis=1)
    imag = np.concatenate([sin, cos], axis=1)
    inner = np.stack(
        [real.reshape(high, LOW, 2 * modes), imag.reshape(high, LOW, 2 * modes)], axis=1
    ).reshape(2 * PHI_T, 2 * modes)
    zero = np.zeros((1, 2 * modes), np.float64)
    edge = np.concatenate([real[LOW::LOW], zero, imag[LOW::LOW], zero], axis=0)
    return jnp.asarray(np.concatenate([inner, edge], axis=0), jnp.bfloat16)


def psi_rows(orders):
    order = np.arange(orders, dtype=np.int64)[:, None]
    cos, sin = wave_table(NPSI, np.arange(NPSI, dtype=np.int64)[None, :], order)
    half = np.concatenate([cos, -sin], axis=0)
    return jnp.asarray(np.concatenate([half, half], axis=1), jnp.bfloat16)


def shards(sky_coeffs, beam_coeffs, wigner, visits, point_slot, phi_cell, psi_cell, fraction):
    order_count = lax.axis_size("order")
    shard_count = lax.axis_size("shard")
    local_modes = sky_coeffs.shape[0]
    local_orders = beam_coeffs.shape[0]
    theta_count = wigner.shape[3]
    orders = local_orders * order_count
    modes = local_modes * shard_count
    lines = shard_count // (SQUARE * CORES)
    if grouped(lines, order_count, modes, orders, visits.shape[1:], point_slot.shape[0], theta_count):
        return run_whole(
            shard_count, sky_coeffs[0], beam_coeffs, wigner[0], visits[0], point_slot, phi_cell, psi_cell, fraction
        )
    weighted = (sky_coeffs[:, None, :, :] * beam_coeffs[None, :, None, :]).astype(jnp.bfloat16)
    coeffs = jnp.einsum("mkcl,mklt->mkct", weighted, wigner, preferred_element_type=jnp.float32)
    coeffs = coeffs.astype(jnp.bfloat16).reshape(local_modes * local_orders * 2, theta_count)
    coeffs = pl.pallas_call(
        functools.partial(gather_blocks, shard_count // (SQUARE * CORES)),
        out_shape=jax.ShapeDtypeStruct((shard_count * coeffs.shape[0], theta_count), jnp.bfloat16),
        in_specs=[pl.BlockSpec(memory_space=pltpu.VMEM)],
        out_specs=pl.BlockSpec(memory_space=pltpu.VMEM),
        scratch_shapes=[
            pltpu.SemaphoreType.DMA((shard_count - 1,)),
            pltpu.SemaphoreType.DMA((shard_count,)),
        ],
        compiler_params=pltpu.CompilerParams(collective_id=0, has_side_effects=True),
    )(coeffs)
    if order_count > 1:
        coeffs = coeffs.reshape(modes, local_orders * 2, theta_count)
        coeffs = lax.all_gather(coeffs, "order", axis=1, tiled=True)
        coeffs = coeffs.reshape(modes * orders * 2, theta_count)

    slots = visits.shape[1] * visits.shape[2]
    count = point_slot.shape[0]
    chunks = count // CHUNK
    lined = (chunks, 1, CHUNK)
    pairs = jnp.transpose(fraction.reshape(2, chunks, CHUNK), (1, 0, 2))
    high = PHI_T // LOW
    timeline = pl.pallas_call(
        functools.partial(
            interpolate, modes, orders, order_count, shard_count
        ),
        out_shape=jax.ShapeDtypeStruct(lined, jnp.float32),
        in_specs=[pl.BlockSpec(memory_space=pltpu.VMEM)] * 8,
        out_specs=pl.BlockSpec(memory_space=pltpu.VMEM),
        scratch_shapes=[
            pltpu.VMEM((modes * orders * 2, LANES), jnp.float32),
            pltpu.VMEM((orders * 2 * high, LANES), jnp.float32),
            pltpu.VMEM((orders * 2 * (LOW + 1), high * slots), jnp.bfloat16),
            pltpu.VMEM((orders * 2, CHUNK), jnp.float32),
            pltpu.VMEM((orders * 2, CHUNK), jnp.float32),
            pltpu.VMEM((orders * 2 * (LOW + 1), CHUNK), jnp.float32),
            pltpu.VMEM((orders * 2 * (LOW + 1), CHUNK), jnp.float32),
        ],
    )(
        coeffs,
        jnp.transpose(visits[0]),
        phi_rows(modes),
        psi_rows(orders),
        point_slot.reshape(lined),
        phi_cell.reshape(lined),
        psi_cell.reshape(lined),
        pairs,
    )
    return timeline.reshape(count)


def solution(mesh):
    placed = (
        P("shard", None, None),
        P("order", None),
        P("shard", "order", None, None),
        P(("order", "shard"), None, None),
        P(("order", "shard")),
        P(("order", "shard")),
        P(("order", "shard")),
        P(None, ("order", "shard")),
    )
    return jax.shard_map(
        shards, mesh=mesh, in_specs=placed, out_specs=P(("order", "shard")), check_vma=False
    )
```

```python
import functools
import math

import jax
import jax.numpy as jnp
import numpy as np
from jax import lax
from jax.experimental import pallas as pl
from jax.experimental.pallas import tpu as pltpu
from jax.sharding import PartitionSpec as P

NPHI = 4096
NPSI = 128
PHI_T = 32
LOW = 8
LANES = 128
CHUNK = 256
KB = 8
BLOCK = 256
F32, BF16, I32 = jnp.float32, jnp.bfloat16, jnp.int32


SQUARE = 4
CORES = 2


def gather_blocks(lines, block_ref, out_ref, send_sem, recv_sem):
    me = lax.axis_index("shard")
    core = me % CORES
    square = me // CORES % SQUARE
    line = me // (CORES * SQUARE)
    depth = block_ref.shape[0]

    def index(at_line, at_square, at_core):
        return (at_line * SQUARE + at_square) * CORES + at_core

    along = [(line + d) % lines for d in range(1, lines)]
    if lines == 4:
        half = line // 2
        along = [line + 1 - 2 * (line % 2), 2 - half, 3 - 3 * half]
    across = [(square + d) % SQUARE for d in range(1, SQUARE)]
    other = (core + 1) % CORES
    line_peers = [index(a, square, core) for a in along]
    square_peers = [index(line, b, core) for b in across]
    twin = index(line, square, other)
    barrier = pltpu.get_barrier_semaphore()
    peers = line_peers + square_peers + [twin]
    for peer in peers:
        pl.semaphore_signal(
            barrier, inc=1, device_id={"shard": peer}, device_id_type=pl.DeviceIdType.MESH
        )
    pl.semaphore_wait(barrier, len(peers))

    started = []

    def place(owner):
        return out_ref.at[pl.ds(pl.multiple_of(owner * depth, depth), depth), :]

    def send(source, owner, peer):
        copy = pltpu.make_async_remote_copy(
            src_ref=source,
            dst_ref=place(owner),
            send_sem=send_sem.at[len(started)],
            recv_sem=recv_sem.at[owner],
            device_id={"shard": peer},
            device_id_type=pl.DeviceIdType.MESH,
        )
        copy.start()
        started.append(copy)

    def arrive(owner):
        pltpu.make_async_remote_copy(
            src_ref=place(owner),
            dst_ref=place(owner),
            send_sem=send_sem.at[0],
            recv_sem=recv_sem.at[owner],
            device_id={"shard": twin},
            device_id_type=pl.DeviceIdType.MESH,
        ).wait_recv()

    for peer in line_peers[::-1] + square_peers + [twin]:
        send(block_ref, me, peer)
    out_ref[pl.ds(pl.multiple_of(me * depth, depth), depth), :] = block_ref[...]
    for owner in line_peers:
        arrive(owner)
        for peer in square_peers + [twin]:
            send(place(owner), owner, peer)
    for a in [line] + along:
        for b in across:
            owner = index(a, b, core)
            arrive(owner)
            send(place(owner), owner, twin)
    for a in [line] + along:
        for b in [square] + across:
            arrive(index(a, b, other))
    for copy in started:
        copy.wait_send()


def wave_table(count, grid, mode):
    phase = 2.0 * math.pi * ((grid * mode) % count) / count
    return np.cos(phase), np.sin(phase)


INSIDE = True
EARLY = True
FINE = True
PARTS = 4
AHEAD = 2
LAG = (3, 5)
NT = (((1,), (1,)), ((), ()))


def grouped(lines, order_count, modes, orders, visits, count, theta):
    owners, depth = visits
    return (
        lines > 1
        and order_count == 1
        and modes == owners
        and orders % KB == 0
        and 2 * orders == theta == owners * depth == PHI_T * depth == NPSI == LANES
        and count % (2 * owners * BLOCK) == 0
        and count == orders * BLOCK
    )


def row_hot(index, size, dtype=BF16):
    n = index.shape[1]
    rows = lax.broadcasted_iota(I32, (size, n), 0)
    if dtype == BF16:
        return rows.astype(F32).astype(BF16) == jnp.broadcast_to(index.astype(F32).astype(BF16), (size, n))
    return rows == index


def pick_row(index, *values):
    size, n = values[0].shape
    totals = [jnp.zeros((8, n), F32) for _ in values]
    index = jnp.broadcast_to(index, (8, n)) - lax.broadcasted_iota(I32, (8, n), 0)
    for r in range(0, size, 8):
        mask = index == r
        totals = [jnp.where(mask, v[r:r + 8], t) for v, t in zip(values, totals)]
    return jnp.sum(functools.reduce(jnp.add, totals), axis=0, keepdims=True)


def block_of(ref, b):
    per = BLOCK // LANES
    return jnp.concatenate([ref[pl.ds(b * per + u, 1), :] for u in range(per)], axis=1)


def mode_order(modes):
    lines = modes // (SQUARE * CORES)
    place = np.arange(modes)
    return (place % lines) * SQUARE * CORES + place // lines % SQUARE * CORES + place // (lines * SQUARE)


def phi_matrix(modes):
    cos, sin = wave_table(NPHI, np.arange(PHI_T)[:, None], mode_order(modes)[None, :])
    core = np.stack([np.stack([cos, -sin], -1), np.stack([sin, cos], -1)], 1)
    full = np.einsum("pamc,kj->pakmcj", core, np.eye(KB))
    return jnp.asarray(full.reshape(PHI_T * 2 * KB, modes * 2 * KB), BF16)


def psi_matrix(orders):
    cos, sin = wave_table(NPSI, np.arange(NPSI)[:, None], np.arange(orders)[None, :])
    pair = np.stack([cos.reshape(NPSI, -1, KB), -sin.reshape(NPSI, -1, KB)], 2)
    return jnp.asarray(pair.reshape(NPSI, 2 * orders), BF16)


def rank_matrix():
    i = np.arange(BLOCK)
    upper = (i[:, None] < i[None, :]).astype(np.float32)
    return jnp.asarray(np.concatenate([upper, np.ones((BLOCK, LANES), np.float32)], 1), BF16)


class Ring:
    def __init__(self, shards, mine, out, send_sem, recv_sem):
        lines = shards // (SQUARE * CORES)
        me = lax.axis_index("shard")
        core, square, line = me % CORES, me // CORES % SQUARE, me // (CORES * SQUARE)
        index = lambda a, b, c: (a * SQUARE + b) * CORES + c
        along = [(line + d) % lines for d in range(1, lines)]
        across = [(square + d) % SQUARE for d in range(1, SQUARE)]
        other = (core + 1) % CORES
        self.shards, self.lines = shards, lines
        self.line_peers = [index(a, square, core) for a in along]
        self.square_peers = [index(line, b, core) for b in across]
        self.twin = index(line, square, other)
        self.all_peers = [
            index(a, b, c) for a in along[::-1] + [line] for b in across[::-1] + [square] for c in (other, core)
        ][:-1]
        self.mine, self.out, self.send_sem, self.recv_sem = mine, out, send_sem, recv_sem
        self.wide = mine.shape[1]
        self.column = core * SQUARE + square
        self.columns = [core * SQUARE + b for b in across]
        self.spot = self.column * lines + line

    def hail(self):
        barrier = pltpu.get_barrier_semaphore()
        for peer in self.all_peers:
            pl.semaphore_signal(barrier, inc=1, device_id={"shard": peer}, device_id_type=pl.DeviceIdType.MESH)

    def meet(self):
        pl.semaphore_wait(pltpu.get_barrier_semaphore(), len(self.all_peers))

    def place(self, j, first, count):
        return self.out.at[j, pl.ds(pl.multiple_of(first * self.wide, self.wide), count * self.wide), :]

    def copy(self, source, target, j, peer, kind):
        return pltpu.make_async_remote_copy(
            src_ref=source,
            dst_ref=target,
            send_sem=self.send_sem.at[j],
            recv_sem=self.recv_sem.at[kind, j],
            device_id={"shard": peer},
            device_id_type=pl.DeviceIdType.MESH,
        )

    def arrive(self, j, kind, blocks):
        span = self.place(j, 0, blocks)
        self.copy(span, span, j, self.twin, kind).wait_recv()

    def sent(self, j, blocks):
        span = self.place(j, 0, blocks)
        self.copy(span, span, j, self.twin, 0).wait_send()

    def first(self, j):
        for peer in self.line_peers:
            self.copy(self.mine.at[j], self.place(j, self.spot, 1), j, peer, 0).start()

    def second(self, j):
        self.arrive(j, 0, self.lines - 1)
        span = self.place(j, self.column * self.lines, self.lines)
        for peer in self.square_peers:
            self.copy(span, span, j, peer, 1).start()
        self.copy(span, span, j, self.twin, 2).start()

    def third(self, j):
        self.arrive(j, 1, (SQUARE - 1) * self.lines)
        for column in self.columns:
            span = self.place(j, column * self.lines, self.lines)
            self.copy(span, span, j, self.twin, 2).start()

    def last(self, j):
        self.arrive(j, 2, SQUARE * self.lines)
        self.sent(j, self.lines - 1)
        self.sent(j, (2 * SQUARE - 1) * self.lines)

    def direct(self, j):
        for peer in self.all_peers:
            self.copy(self.mine.at[j], self.place(j, self.spot, 1), j, peer, 0).start()

    def direct_end(self, j):
        self.arrive(j, 0, self.shards - 1)

    def direct_sent(self, j):
        self.sent(j, self.shards - 1)


def whole_kernel(
    shards, owners, depth,
    sky_hbm, beam_hbm, wigner_hbm, visit_hbm, slot_hbm, phi_hbm, psi_hbm, fraction_hbm, phi_mat_hbm, psi_mat_hbm, rank_hbm,
    out_ref,
    sky, beam, wigner, visit, slot, phi, psi, fraction, phi_mat, psi_mat, rank_mat,
    gathered, mine, turn_cos, turn_sin, dest, carry, chunk_vmem, chunk_smem, moved, hot, weights, aims, synth, lines, table, found, found_both, *rest,
):
    *buffers, load_sem, small_sem, chunk_sem, send_sem, recv_sem = rest
    steps, wide = mine.shape[0], mine.shape[1]
    modes = shards
    theta = wigner.shape[2]
    slots = owners * depth
    blocks = found.shape[0]
    tiles = NPHI // PHI_T
    ring = Ring(shards, mine, gathered, send_sem, recv_sem)

    small = [
        (sky_hbm, sky), (beam_hbm, beam), (slot_hbm, slot), (visit_hbm, visit), (rank_hbm, rank_mat),
        (phi_hbm, phi), (psi_hbm, psi), (fraction_hbm, fraction), (phi_mat_hbm, phi_mat), (psi_mat_hbm, psi_mat),
    ]
    small = [pltpu.make_async_copy(s, d, small_sem.at[n]) for n, (s, d) in enumerate(small)]

    def load(j):
        rows = pl.ds(j * KB, KB)
        return pltpu.make_async_copy(wigner_hbm.at[rows], wigner.at[rows], load_sem.at[j])

    for copy in small[:4]:
        copy.start()
    load(0).start()
    for copy in small[4:]:
        copy.start()
    ahead = AHEAD
    if EARLY:
        for j in range(1, ahead):
            load(j).start()
    ring.hail()

    small[2].wait()

    def own(b):
        owner = block_of(slot, b) >> int(math.log2(depth))
        return lax.broadcasted_iota(I32, (owners, BLOCK), 0) == owner

    def count(b, total):
        return total + jnp.where(own(b), 1, 0)

    total = lax.fori_loop(0, blocks, count, jnp.zeros((owners, BLOCK), I32), unroll=8)
    held = jnp.broadcast_to(jnp.sum(total, axis=1, keepdims=True), (owners, LANES))
    place = lax.broadcasted_iota(I32, (owners, LANES), 0)
    start = jnp.zeros((owners, LANES), I32)
    for o in range(owners - 1):
        start = start + jnp.where(place > o, jnp.broadcast_to(held[o:o + 1], (owners, LANES)), 0)
    lane = lax.broadcasted_iota(I32, (owners, LANES), 1) * BLOCK
    chunk_vmem[...] = jnp.sum(jnp.where(start + held <= lane, 1, 0), axis=0, keepdims=True)
    carry[...] = start.astype(F32)
    tell = pltpu.make_async_copy(chunk_vmem, chunk_smem, chunk_sem)
    tell.start()

    small[3].wait()
    tile = jnp.maximum(jnp.concatenate([visit[d:d + 1, :] for d in range(depth)], axis=1), 0)
    owner = lax.broadcasted_iota(I32, (1, slots), 1) % owners
    row = owner * (theta // owners) + tile // tiles
    first_phi = (tile % tiles) * PHI_T
    pick = jnp.where(row_hot(row, theta, F32), 1.0, 0.0).astype(BF16)
    spot = lax.broadcasted_iota(I32, (modes, slots), 0)
    n_lines = ring.lines
    mode = (spot % n_lines) * (SQUARE * CORES) + spot // n_lines % SQUARE * CORES + spot // (n_lines * SQUARE)
    angle = ((mode * first_phi) % NPHI).astype(F32) * (2.0 * math.pi / NPHI)
    turn_cos[...] = jnp.cos(angle)
    turn_sin[...] = jnp.sin(angle)
    moved[...] = jnp.zeros_like(moved)
    for copy in small[:2] + small[4:]:
        copy.wait()

    per = blocks // steps

    def rank(i):
        source = jnp.minimum(i, steps - 1)
        masks = [own(source * per + u) for u in range(per)]
        stacked = jnp.concatenate([jnp.where(m, 1.0, 0.0).astype(BF16) for m in masks], axis=0)
        seen = jnp.dot(stacked, rank_mat[...], preferred_element_type=F32)
        base = carry[...]
        for u, mask in enumerate(masks):
            part = seen[u * owners:(u + 1) * owners]
            spots = part[:, :BLOCK] + jnp.concatenate([base] * (BLOCK // LANES), axis=1)
            total = jnp.zeros((8, BLOCK), F32)
            for r in range(0, owners, 8):
                total = jnp.where(mask[r:r + 8], spots[r:r + 8], total)
            dest[pl.ds(i * per + u, 1), :] = jnp.sum(total, axis=0, keepdims=True).astype(I32)
            base = base + part[:, BLOCK:]
        carry[...] = base

    hots = [jnp.ones((BLOCK, BLOCK), BF16), jnp.zeros((BLOCK, BLOCK), BF16)]

    def move(b, to):
        at = block_of(phi, b) * depth + (block_of(slot, b) & (depth - 1))
        mask = row_hot(to >> 8, blocks)
        span = pl.ds(pl.multiple_of(b * BLOCK, BLOCK), BLOCK)
        parts = [at.astype(F32), block_of(psi, b).astype(F32), fraction[0:1, span], fraction[1:2, span]]
        zero = jnp.zeros((blocks, BLOCK), BF16)
        rows = jnp.concatenate(
            [jnp.where(mask, jnp.broadcast_to(p.astype(BF16), (blocks, BLOCK)), zero) for p in parts], axis=0)
        lanes = jnp.where(row_hot(to & 255, BLOCK), *hots)
        hot[span, :] = lanes
        return lax.dot_general(rows, lanes, NT, preferred_element_type=F32)

    size = PHI_T * depth

    def weight(c, s):
        at, along = moved[pl.ds(c, 1), :], moved[pl.ds(2 * blocks + c, 1), :]
        wide_row = lambda w: jnp.broadcast_to(w.astype(BF16), (size, BLOCK))
        both = jnp.where(
            row_hot(at, size), wide_row(1.0 - along),
            jnp.where(row_hot(at + depth, size), wide_row(along), jnp.zeros((size, BLOCK), BF16)))
        weights[pl.ds(pl.multiple_of(c * size, size), size), :] = both
        angle, across = moved[pl.ds(blocks + c, 1), :], moved[pl.ds(3 * blocks + c, 1), :]
        after = jnp.where(angle == NPSI - 1, 0.0, angle + 1.0)
        aims[pl.ds(pl.multiple_of(c * NPSI, NPSI), NPSI), :] = jnp.where(
            row_hot(angle, NPSI), wide_row(1.0 - across),
            jnp.where(row_hot(after, NPSI), wide_row(across), jnp.zeros((NPSI, BLOCK), BF16)))
        return s

    def weigh(j, others):
        part = beam[pl.ds(pl.multiple_of(j * KB, KB), KB), :]
        rows = jnp.concatenate([sky[c:c + 1, :] * part for c in range(2)], axis=0)
        rows = rows.astype(BF16)
        kind = lax.broadcasted_iota(I32, (2 * KB, theta), 0) % KB
        total = jnp.zeros((2 * KB, theta), F32)
        gain = moved[...]
        for kk in range(0, KB, 2):
            pair = jnp.concatenate([wigner[j * KB + kk], wigner[j * KB + kk + 1]], axis=1)
            both = jnp.dot(rows, pair, preferred_element_type=F32)
            for u in range(2):
                total = jnp.where(kind == kk + u, both[:, u * theta:(u + 1) * theta], total)
            for other in others[kk * len(others) // KB:(kk + 2) * len(others) // KB]:
                gain = gain + move(*other)
        moved[...] = gain
        block = total.astype(BF16)
        mine[j] = block
        gathered[j, pl.ds(pl.multiple_of(ring.spot * wide, wide), wide), :] = block

    def synthesize(j, width):
        sides = []
        for w in range(width):
            x = jnp.dot(gathered[j + w], pick, preferred_element_type=F32)
            turned = []
            for m in range(modes):
                re, im = x[m * wide:m * wide + KB], x[m * wide + KB:(m + 1) * wide]
                cm, sm = turn_cos[pl.ds(m, KB, stride=0), :], turn_sin[pl.ds(m, KB, stride=0), :]
                turned.append(jnp.concatenate([cm * re - sm * im, sm * re + cm * im], axis=0).astype(BF16))
            sides.append(jnp.concatenate(turned, axis=0))
        y = jnp.dot(phi_mat[...], jnp.concatenate(sides, axis=1), preferred_element_type=F32)
        for w in range(width):
            for p in range(PHI_T):
                synth[p, pl.ds(pl.multiple_of((j + w) * wide, wide), wide), :] = y[
                    p * wide:(p + 1) * wide, w * slots:(w + 1) * slots].astype(BF16)

    lag = LAG

    def step(i, c):
        load(i).wait()

        @pl.when(i + ahead < steps)
        def _():
            load(i + ahead).start()

        goals = [dest[pl.ds(i * per + u, 1), :] for u in range(per)]
        rank(i + 1)
        weigh(i, [(i * per + u, goal) for u, goal in enumerate(goals)])

        if INSIDE:
            @pl.when(i == 0)
            def _():
                ring.meet()

        @pl.when(i >= lag[0])
        def _():
            ring.second(i - lag[0])

        @pl.when(i >= lag[1])
        def _():
            ring.third(i - lag[1])

        @pl.when(i < steps - 1)
        def _():
            ring.first(i)

        @pl.when(i == steps - 1)
        def _():
            ring.direct(i)
        return c

    if not EARLY:
        for j in range(1, ahead):
            load(j).start()
    rank(0)
    if not INSIDE:
        ring.meet()
    lax.fori_loop(0, steps, step, 0)
    end = steps - 1
    waits = [(j * 1.5 + 3.75, ring.second, j) for j in range(steps - lag[0], end)]
    waits += [(j * 1.5 + 6.5, ring.third, j) for j in range(steps - lag[1], end)]
    waits.sort(key=lambda w: (w[0], w[2]))
    part = blocks // PARTS
    for n in range(PARTS):
        lax.fori_loop(n * part, (n + 1) * part, weight, 0, unroll=4)
        for _, wait, j in waits[n * len(waits) // PARTS:(n + 1) * len(waits) // PARTS]:
            wait(j)

    def early(j, c):
        ring.last(2 * j)
        ring.last(2 * j + 1)
        synthesize(2 * j, 2)
        return c

    lax.fori_loop(0, end // 2, early, 0)
    if end % 2:
        ring.last(end - 1)
        synthesize(end - 1, 1)
    tell.wait()
    ring.direct_end(end)
    synthesize(end, 1)
    spots = lax.broadcasted_iota(I32, (2 * slots, 2 * slots), 0)
    from_spot = spots // depth % 2 * slots + spots % depth * owners + spots // (2 * depth)
    shuffle = (
        lax.broadcasted_iota(I32, (2 * slots, 2 * slots), 1) == from_spot
    ).astype(F32).astype(BF16)

    def flip(q, c):
        pairs = [
            jnp.concatenate([synth[4 * q + 2 * u], synth[4 * q + 2 * u + 1]], axis=1) for u in range(2)
        ]
        turned = lax.dot_general(shuffle, jnp.concatenate(pairs, axis=0), NT, preferred_element_type=F32)
        rows = 2 * depth
        for o in range(owners):
            for u in range(2):
                lines[pl.ds(pl.multiple_of(o * slots + (2 * q + u) * rows, rows), rows), :] = turned[
                    o * rows:(o + 1) * rows, u * LANES:(u + 1) * LANES]
        return c

    lax.fori_loop(0, PHI_T // 4, flip, 0, unroll=2)

    def cube(p, c):
        part = lines[pl.ds(pl.multiple_of(2 * p * slots, 2 * slots), 2 * slots), :].astype(BF16)
        both = lax.dot_general(psi_mat[...], part, NT, preferred_element_type=F32).astype(BF16)
        for u in range(2):
            table[2 * p + u] = both[:, u * LANES:(u + 1) * LANES]
        return c

    lax.fori_loop(0, owners // 2, cube, 0, unroll=8)
    def meet(c, buffer):
        o = chunk_smem[0, c]
        w = weights[pl.ds(pl.multiple_of(c * size, size), size), :]
        buffer[...] = jnp.dot(table[o], w, preferred_element_type=F32)

    def choose(c, buffer):
        aim = aims[pl.ds(pl.multiple_of(c * NPSI, NPSI), NPSI), :].astype(F32)
        total = jnp.zeros((8, BLOCK), F32)
        for r in range(0, NPSI, 8):
            total = total + buffer[r:r + 8, :] * aim[r:r + 8]
        found[pl.ds(c, 1), :] = jnp.sum(total, axis=0, keepdims=True)

    def pipeline(count, begin, finish, buffers):
        deep = len(buffers) // 2
        for u in range(deep):
            begin(u, buffers[u])

        def both(i, s):
            for side in range(2):
                now = (2 * i + side) * deep
                ahead = jnp.minimum(now + deep, count - deep)
                for u in range(deep):
                    begin(ahead + u, buffers[(1 - side) * deep + u])
                    finish(now + u, buffers[side * deep + u])
            return s

        lax.fori_loop(0, count // (2 * deep), both, 0)

    pipeline(blocks, meet, choose, buffers)
    values = found[...]
    coarse = values.astype(BF16)
    if FINE:
        found_both[...] = jnp.concatenate([coarse, (values - coarse.astype(F32)).astype(BF16)], axis=0)
    else:
        found_both[0:blocks] = coarse

    def spread(b, buffer):
        lanes = hot[pl.ds(pl.multiple_of(b * BLOCK, BLOCK), BLOCK), :]
        height = 2 * blocks if FINE else blocks
        buffer[0:height] = jnp.dot(found_both[0:height], lanes, preferred_element_type=F32)

    def settle(b, buffer):
        parts = [buffer.at[0:blocks], buffer.at[blocks:2 * blocks]] if FINE else [buffer.at[0:blocks]]
        line = pick_row(dest[pl.ds(b, 1), :] >> 8, *parts)
        for u in range(BLOCK // LANES):
            out_ref[pl.ds(b * (BLOCK // LANES) + u, 1), :] = line[:, u * LANES:(u + 1) * LANES]

    pipeline(blocks, spread, settle, buffers)
    ring.direct_sent(end)


def run_whole(shards, sky, beam, wigner, visits, point_slot, phi_cell, psi_cell, fraction):
    orders, length, theta = wigner.shape
    owners, depth = visits.shape
    count = point_slot.shape[0]
    blocks = count // BLOCK
    steps, wide = orders // KB, 2 * KB
    slots = owners * depth
    lined = (blocks, BLOCK)
    args = (
        sky, beam, wigner, jnp.transpose(visits), point_slot.reshape(-1, LANES), phi_cell.reshape(-1, LANES),
        psi_cell.reshape(-1, LANES), fraction, phi_matrix(shards), psi_matrix(orders), rank_matrix(),
    )
    return pl.pallas_call(
        functools.partial(whole_kernel, shards, owners, depth),
        out_shape=jax.ShapeDtypeStruct((count // LANES, LANES), F32),
        in_specs=[pl.BlockSpec(memory_space=pl.ANY)] * len(args),
        out_specs=pl.BlockSpec(memory_space=pltpu.VMEM),
        scratch_shapes=[pltpu.VMEM(a.shape, a.dtype) for a in args] + [
            pltpu.VMEM((steps, shards * wide, theta), BF16),
            pltpu.VMEM((steps, wide, theta), BF16),
            pltpu.VMEM((shards, slots), F32),
            pltpu.VMEM((shards, slots), F32),
            pltpu.VMEM((blocks + blocks // steps, BLOCK), I32),
            pltpu.VMEM((owners, LANES), F32),
            pltpu.VMEM((1, LANES), I32),
            pltpu.SMEM((1, LANES), I32),
            pltpu.VMEM((4 * blocks, BLOCK), F32),
            pltpu.VMEM((blocks * BLOCK, BLOCK), BF16),
            pltpu.VMEM((blocks * PHI_T * depth, BLOCK), BF16),
            pltpu.VMEM((blocks * NPSI, BLOCK), BF16),
            pltpu.VMEM((PHI_T, 2 * orders, slots), BF16),
            pltpu.VMEM((PHI_T * slots, 2 * orders), F32),
            pltpu.VMEM((owners, NPSI, LANES), BF16),
            pltpu.VMEM(lined, F32),
            pltpu.VMEM((2 * blocks, BLOCK), BF16),
            *[pltpu.VMEM((max(NPSI, 2 * blocks), BLOCK), F32)] * 8,
            pltpu.SemaphoreType.DMA((steps,)),
            pltpu.SemaphoreType.DMA((len(args) - 1,)),
            pltpu.SemaphoreType.DMA,
            pltpu.SemaphoreType.DMA((steps,)),
            pltpu.SemaphoreType.DMA((3, steps)),
        ],
        compiler_params=pltpu.CompilerParams(collective_id=1, has_side_effects=True, vmem_limit_bytes=67043328),
        name="timeline",
    )(*args).reshape(count)


def interpolate(
    modes,
    orders,
    order_count,
    shard_count,
    coeffs_ref,
    visit_ref,
    phi_table_ref,
    psi_table_ref,
    slot_ref,
    phi_ref,
    psi_ref,
    fraction_ref,
    out_ref,
    picked,
    edge,
    synth,
    wave_a,
    wave_b,
    values_a,
    values_b,
):
    terms = 2 * orders
    high = PHI_T // LOW
    theta = coeffs_ref.shape[1]
    depth, owners = visit_ref.shape
    slots = owners * depth
    blocks = NPHI // (order_count * PHI_T)
    groups = slots // LANES
    listed = jnp.concatenate([visit_ref[d : d + 1, :] for d in range(depth)], axis=1)
    for g in range(groups):
        lanes = slice(g * LANES, (g + 1) * LANES)
        tile = jnp.maximum(listed[:, lanes], 0)
        owner = (lax.broadcasted_iota(jnp.int32, (1, LANES), 1) + g * LANES) % owners
        row = (owner % shard_count) * (theta // shard_count) + tile // blocks
        first_phi = (owner // shard_count) * (NPHI // order_count) + (tile % blocks) * PHI_T
        chosen = (
            lax.broadcasted_iota(jnp.int32, (theta, LANES), 0) == row
        ).astype(jnp.float32).astype(jnp.bfloat16)

        def pick(m, carry):
            rows = pl.ds(pl.multiple_of(m * 4 * terms, 4 * terms), 4 * terms)
            picked[rows, :] = jnp.dot(
                coeffs_ref[rows, :], chosen, preferred_element_type=jnp.float32
            )
            return carry

        lax.fori_loop(0, modes // 4, pick, 0)
        turn = (lax.broadcasted_iota(jnp.int32, (modes, LANES), 0) * first_phi) % NPHI
        angle = turn.astype(jnp.float32) * (2.0 * math.pi / NPHI)
        turn_cos, turn_sin = jnp.cos(angle), jnp.sin(angle)

        def sum_modes(k, carry):
            real = picked[pl.ds(2 * k, modes, stride=terms), :]
            imag = picked[pl.ds(2 * k + 1, modes, stride=terms), :]
            turned = jnp.concatenate(
                [turn_cos * real - turn_sin * imag, turn_sin * real + turn_cos * imag], axis=0
            ).astype(jnp.bfloat16)
            values = jnp.dot(phi_table_ref[...], turned, preferred_element_type=jnp.float32)
            for h in range(high):
                synth[
                    pl.ds(pl.multiple_of(k * 2 * LOW, 2 * LOW), 2 * LOW),
                    h * slots + g * LANES : h * slots + (g + 1) * LANES,
                ] = values[h * 2 * LOW : (h + 1) * 2 * LOW].astype(jnp.bfloat16)
            edge[pl.ds(pl.multiple_of(k * 2 * high, 2 * high), 2 * high), :] = values[
                2 * PHI_T :
            ]
            return carry

        lax.fori_loop(0, orders, sum_modes, 0, unroll=4)
        for part in range(2):
            for h in range(high):
                synth[
                    terms * LOW + part * orders : terms * LOW + (part + 1) * orders,
                    h * slots + g * LANES : h * slots + (g + 1) * LANES,
                ] = edge[pl.ds(part * high + h, orders, stride=2 * high), :].astype(jnp.bfloat16)

    def begin(i, values, wave):
        phi, psi = phi_ref[i], psi_ref[i]
        along_psi = fraction_ref[i][1:2]
        slot = slot_ref[i]
        key = ((phi // LOW) * depth + slot % depth) * owners + slot // depth
        entry = (
            lax.broadcasted_iota(jnp.int32, (high * slots, CHUNK), 0) == key
        ).astype(jnp.float32).astype(jnp.bfloat16)
        at_psi = lax.broadcasted_iota(jnp.int32, (NPSI, CHUNK), 0)
        weight = jnp.where(
            at_psi == psi, 1.0 - along_psi, jnp.where(at_psi == (psi + 1) % NPSI, along_psi, 0.0)
        )
        coarse = weight.astype(jnp.bfloat16)
        fine = (weight - coarse.astype(jnp.float32)).astype(jnp.bfloat16)
        wave[...] = jnp.dot(
            psi_table_ref[...],
            jnp.concatenate([coarse, fine], axis=0),
            preferred_element_type=jnp.float32,
        )
        values[...] = jnp.dot(synth[...], entry, preferred_element_type=jnp.float32)

    def finish(i, values, wave):
        phi = phi_ref[i]
        along_phi = fraction_ref[i][0:1]
        sums = [jnp.zeros((LOW, CHUNK), jnp.float32) for _ in range(4)]
        for k in range(orders):
            for part in range(2):
                at = (2 * k + part) * LOW
                line = part * orders + k
                sums[at // LOW % 4] += values[at : at + LOW, :] * wave[line : line + 1, :]
        inner = (sums[0] + sums[1]) + (sums[2] + sums[3])
        last = jnp.sum(values[terms * LOW :, :] * wave[...], axis=0, keepdims=True)
        low = phi % LOW
        at_low = lax.broadcasted_iota(jnp.int32, (LOW, CHUNK), 0)
        weight_phi = jnp.where(
            at_low == low, 1.0 - along_phi, jnp.where(at_low == low + 1, along_phi, 0.0)
        )
        total = jnp.sum(inner * weight_phi, axis=0, keepdims=True)
        out_ref[i] = total + jnp.where(low == LOW - 1, along_phi, 0.0) * last

    chunks = slot_ref.shape[0]
    begin(0, values_a, wave_a)

    def pair(i, carry):
        begin(2 * i + 1, values_b, wave_b)
        finish(2 * i, values_a, wave_a)
        begin(jnp.minimum(2 * i + 2, chunks - 1), values_a, wave_a)
        finish(2 * i + 1, values_b, wave_b)
        return carry

    lax.fori_loop(0, chunks // 2, pair, 0)


def phi_rows(modes):
    mode = np.arange(modes, dtype=np.int64)[None, :]
    high = PHI_T // LOW
    cos, sin = wave_table(NPHI, np.arange(PHI_T, dtype=np.int64)[:, None], mode)
    real = np.concatenate([cos, -sin], axis=1)
    imag = np.concatenate([sin, cos], axis=1)
    inner = np.stack(
        [real.reshape(high, LOW, 2 * modes), imag.reshape(high, LOW, 2 * modes)], axis=1
    ).reshape(2 * PHI_T, 2 * modes)
    zero = np.zeros((1, 2 * modes), np.float64)
    edge = np.concatenate([real[LOW::LOW], zero, imag[LOW::LOW], zero], axis=0)
    return jnp.asarray(np.concatenate([inner, edge], axis=0), jnp.bfloat16)


def psi_rows(orders):
    order = np.arange(orders, dtype=np.int64)[:, None]
    cos, sin = wave_table(NPSI, np.arange(NPSI, dtype=np.int64)[None, :], order)
    half = np.concatenate([cos, -sin], axis=0)
    return jnp.asarray(np.concatenate([half, half], axis=1), jnp.bfloat16)


def shards(sky_coeffs, beam_coeffs, wigner, visits, point_slot, phi_cell, psi_cell, fraction):
    order_count = lax.axis_size("order")
    shard_count = lax.axis_size("shard")
    local_modes = sky_coeffs.shape[0]
    local_orders = beam_coeffs.shape[0]
    theta_count = wigner.shape[3]
    orders = local_orders * order_count
    modes = local_modes * shard_count
    lines = shard_count // (SQUARE * CORES)
    if grouped(lines, order_count, modes, orders, visits.shape[1:], point_slot.shape[0], theta_count):
        return run_whole(
            shard_count, sky_coeffs[0], beam_coeffs, wigner[0], visits[0], point_slot, phi_cell, psi_cell, fraction
        )
    weighted = (sky_coeffs[:, None, :, :] * beam_coeffs[None, :, None, :]).astype(jnp.bfloat16)
    coeffs = jnp.einsum("mkcl,mklt->mkct", weighted, wigner, preferred_element_type=jnp.float32)
    coeffs = coeffs.astype(jnp.bfloat16).reshape(local_modes * local_orders * 2, theta_count)
    coeffs = pl.pallas_call(
        functools.partial(gather_blocks, shard_count // (SQUARE * CORES)),
        out_shape=jax.ShapeDtypeStruct((shard_count * coeffs.shape[0], theta_count), jnp.bfloat16),
        in_specs=[pl.BlockSpec(memory_space=pltpu.VMEM)],
        out_specs=pl.BlockSpec(memory_space=pltpu.VMEM),
        scratch_shapes=[
            pltpu.SemaphoreType.DMA((shard_count - 1,)),
            pltpu.SemaphoreType.DMA((shard_count,)),
        ],
        compiler_params=pltpu.CompilerParams(collective_id=0, has_side_effects=True),
    )(coeffs)
    if order_count > 1:
        coeffs = coeffs.reshape(modes, local_orders * 2, theta_count)
        coeffs = lax.all_gather(coeffs, "order", axis=1, tiled=True)
        coeffs = coeffs.reshape(modes * orders * 2, theta_count)

    slots = visits.shape[1] * visits.shape[2]
    count = point_slot.shape[0]
    chunks = count // CHUNK
    lined = (chunks, 1, CHUNK)
    pairs = jnp.transpose(fraction.reshape(2, chunks, CHUNK), (1, 0, 2))
    high = PHI_T // LOW
    timeline = pl.pallas_call(
        functools.partial(
            interpolate, modes, orders, order_count, shard_count
        ),
        out_shape=jax.ShapeDtypeStruct(lined, jnp.float32),
        in_specs=[pl.BlockSpec(memory_space=pltpu.VMEM)] * 8,
        out_specs=pl.BlockSpec(memory_space=pltpu.VMEM),
        scratch_shapes=[
            pltpu.VMEM((modes * orders * 2, LANES), jnp.float32),
            pltpu.VMEM((orders * 2 * high, LANES), jnp.float32),
            pltpu.VMEM((orders * 2 * (LOW + 1), high * slots), jnp.bfloat16),
            pltpu.VMEM((orders * 2, CHUNK), jnp.float32),
            pltpu.VMEM((orders * 2, CHUNK), jnp.float32),
            pltpu.VMEM((orders * 2 * (LOW + 1), CHUNK), jnp.float32),
            pltpu.VMEM((orders * 2 * (LOW + 1), CHUNK), jnp.float32),
        ],
    )(
        coeffs,
        jnp.transpose(visits[0]),
        phi_rows(modes),
        psi_rows(orders),
        point_slot.reshape(lined),
        phi_cell.reshape(lined),
        psi_cell.reshape(lined),
        pairs,
    )
    return timeline.reshape(count)


def solution(mesh):
    placed = (
        P("shard", None, None),
        P("order", None),
        P("shard", "order", None, None),
        P(("order", "shard"), None, None),
        P(("order", "shard")),
        P(("order", "shard")),
        P(("order", "shard")),
        P(None, ("order", "shard")),
    )
    return jax.shard_map(
        shards, mesh=mesh, in_specs=placed, out_specs=P(("order", "shard")), check_vma=False
    )
```
